32 devices in a mesh: dp: 16 (over z, y, x), segment: 2 (over core).
Axes of the slice: x: 2, y: 2, z: 4, core: 2. Of those that a mesh axis runs over, the one named last changes fastest.
Arguments:
- latents: bfloat16 [16384, 640], P('dp'), may hold values from -6 to 6
- noise: bfloat16 [16384, 640], P('dp'), may hold values from -6 to 6
- timesteps: int32 [128], P('dp'), may hold values from 100 to 799
- reward_dir: float32 [640], replicated, may hold values from -6 to 6
- gain: float32 [2, 640], P('segment'), may hold values from 0.5 to 1.5
- time_scale: float32 [2, 640], P('segment'), may hold values from -6 to 6
- w_in: bfloat16 [2, 640, 640], P('segment', 'dp'), may hold values from -0.25 to 0.25
- w_out: bfloat16 [2, 640, 640], P('segment', 'dp'), may hold values from -0.25 to 0.25
Outputs:
- weight_grads: float32 [2, 640, 1280], P('segment', 'dp')
The draws below stay inside these ranges and needn't reach their ends.
All inputs are finite; a program needn't handle non-finite values.
Results may differ from the reference program's by a relative error of at most 0.0004.
Values may be sent and summed in bfloat16 or wider, within the bound.
A program may use at most 64 MiB of HBM per device.

```python
import math
import jax
import jax.numpy as jnp
from jax import lax

C = 640
GROUPS = 32
NSTEPS = 1000
STRIDE = 20
MICRO = 8
ROWS_MB = 128
SEGMENTS = 2
IMAGES = 128
ROWS = 16384
N_DP = 16
N_SEGMENT = 2


def plant(array, stream_key, smallest, largest):
    longest = array.shape.index(max(array.shape))
    spots = []
    for shift in (0, 1):
        where = [jax.random.randint(jax.random.fold_in(stream_key, axis), (), 0, length) for axis, length in enumerate(array.shape)]
        where[longest] = (where[longest] + shift) % array.shape[longest]
        spots.append(tuple(where))
    return array.at[spots[0]].set(smallest).at[spots[1]].set(largest)


def raised(values, own_key, source, target, blocks, factor):
    def block_of(position):
        return (jnp.arange(values.shape[position]) // (values.shape[position] // blocks)).reshape((-1,) + (1,) * (values.ndim - 1 - position))

    near = jax.random.permutation(own_key, blocks)[block_of(target)]
    other_side = (block_of(target) + blocks // 2) % blocks
    return jnp.where((block_of(source) == near) | (block_of(source) == other_side), factor * values, values)


def level_of(own_key, shape, shards, low, high):
    level, own = 1.0, jax.random.fold_in(own_key, 6)
    for dim, blocks in shards:
        draws = jnp.exp(jax.random.uniform(jax.random.fold_in(own, dim), (blocks,), jnp.float32, low / len(shards), high / len(shards)))
        level = level * jnp.repeat(draws, shape[dim] // blocks).reshape([-1 if axis == dim else 1 for axis in range(len(shape))])
    return level


def scatter_about(rng, shape, spread, bound, pieces=(), kind=jnp.bfloat16):
    values = jax.random.normal(rng, shape, jnp.float32) * spread
    if len(pieces) > 0:
        values = level_of(rng, shape, pieces, -0.22, 0.18) * values
    return jnp.clip(values, min=-bound, max=bound).astype(kind)


def gaussian_with(key, extent, width, most, split, heavy, held_as=jnp.bfloat16):
    drawn = width * jax.random.normal(key, extent, jnp.float32)
    if split:
        drawn = drawn * level_of(key, extent, split, -0.22, 0.18)
    return jnp.clip(raised(drawn, jax.random.fold_in(key, 3), *heavy), -most, most).astype(held_as)


def setup_inputs(seed: int = 0) -> dict:
    arg_keys = jax.random.split(jax.random.key(seed), 9)
    latents = gaussian_with(arg_keys[0], (ROWS, C), 1.0, 6.0, ((0, 16),), (0, 1, 16, 2.0))
    noise = scatter_about(arg_keys[1], (ROWS, C), 1.0, 6.0, ((0, 16),))
    timesteps = plant(jax.random.randint(arg_keys[2], (IMAGES,), 100, 800), jax.random.fold_in(arg_keys[2], 1), 100, 799).astype(jnp.int32)
    reward_dir = scatter_about(arg_keys[3], (C,), 1.0, 6.0, (), jnp.float32)
    gain = jnp.clip(0.5 + 1.0 * jax.random.uniform(arg_keys[4], (SEGMENTS, C), jnp.float32) ** level_of(arg_keys[4], (SEGMENTS, C), ((0, 2),), -0.2, 0.2), 0.5, 1.5)
    time_scale = scatter_about(arg_keys[5], (SEGMENTS, C), 1.0, 6.0, ((0, 2),), jnp.float32)
    w_in = scatter_about(arg_keys[6], (SEGMENTS, C, C), C ** -0.5, 0.25, ((0, 2), (1, 16)))
    w_out = scatter_about(arg_keys[7], (SEGMENTS, C, C), C ** -0.5, 0.25, ((0, 2), (1, 16)))
    return {"latents": latents, "noise": noise, "timesteps": timesteps, "reward_dir": reward_dir, "gain": gain, "time_scale": time_scale, "w_in": w_in, "w_out": w_out}


EPS = 1e-05

def group_norm(state_f32, group_count):
    channels = state_f32.shape[1]
    per_group = channels // group_count
    col_mean = lax.optimization_barrier(jnp.mean(state_f32, axis=0))
    group_mean = jnp.repeat(lax.optimization_barrier(jnp.mean(col_mean.reshape(group_count, per_group), axis=1)), per_group)
    centered = state_f32 - group_mean
    sq_mean = lax.optimization_barrier(jnp.mean(centered * centered, axis=0))
    variance = jnp.repeat(lax.optimization_barrier(jnp.mean(sq_mean.reshape(group_count, per_group), axis=1)), per_group)
    return centered * lax.rsqrt(variance + EPS)

def time_embed(timestep, channels):
    half_width = channels // 2
    frequencies = jnp.exp(-math.log(10000.0) * jnp.arange(half_width).astype(jnp.float32) / half_width)
    phases = timestep.astype(jnp.float32) * frequencies
    return jnp.concatenate([jnp.sin(phases), jnp.cos(phases)])

def alpha_bar(timestep):
    value = ((timestep.astype(jnp.float32) + 1.0) / NSTEPS + 0.008) / 1.008 * (math.pi / 2.0)
    return jnp.cos(value) ** 2

def contract_rows(left, right):
    return lax.dot_general(left, right, (((0,), (0,)), ((), ())), preferred_element_type=jnp.float32)

def contract_cols(left, right):
    return lax.dot_general(left, right, (((1,), (1,)), ((), ())), preferred_element_type=jnp.float32)

def block_forward(hidden, gain_row, temb, first, second):
    state_f32 = hidden.astype(jnp.float32)
    normed = (group_norm(state_f32, GROUPS) * gain_row).astype(jnp.bfloat16)
    preact = jnp.dot(normed, first, preferred_element_type=jnp.float32) + temb
    activation = jax.nn.silu(preact).astype(jnp.bfloat16)
    result = (state_f32 + jnp.dot(activation, second, preferred_element_type=jnp.float32)).astype(jnp.bfloat16)
    return (result, normed, preact, activation)

def block_backward(hidden, gain_row, preact, cotangent, first, second):
    grad_act = contract_cols(cotangent, second)
    gate_value = jax.nn.sigmoid(preact)
    grad_pre = (grad_act * gate_value * (1.0 + preact * (1.0 - gate_value))).astype(jnp.bfloat16)
    grad_norm = contract_cols(grad_pre, first)
    _, pullback = jax.vjp(lambda values: group_norm(values, GROUPS), hidden.astype(jnp.float32))
    new_cot = (cotangent.astype(jnp.float32) + pullback(grad_norm * gain_row)[0]).astype(jnp.bfloat16)
    return (new_cot, grad_pre)

def weight_term(normed, grad_pre, activation, cotangent):
    return jnp.concatenate([contract_rows(normed, grad_pre), contract_rows(activation, cotangent)], axis=1)

def sample_head(hidden, latent, noise_block, timestep, reward_dir, loss_scale):
    ab_now = alpha_bar(timestep)
    ab_prev = alpha_bar(timestep - STRIDE)
    coef_a = jnp.sqrt(ab_now)
    coef_b = jnp.sqrt(1.0 - ab_now)
    coef_p = jnp.sqrt(ab_prev)
    coef_q = jnp.sqrt(0.75 * (1.0 - ab_prev))
    coef_r = 0.5 * jnp.sqrt(1.0 - ab_prev)
    noise_pred, pullback = jax.vjp(lambda values: group_norm(values, GROUPS), hidden.astype(jnp.float32))
    current = latent.astype(jnp.float32)
    previous = coef_p * (current - coef_b * noise_pred) / coef_a + coef_q * noise_pred + coef_r * noise_block.astype(jnp.float32)
    squashed = jnp.tanh(previous)
    grad_pred = (coef_q - coef_p * coef_b / coef_a) * reward_dir * (1.0 - squashed * squashed) * loss_scale
    return pullback(grad_pred)[0].astype(jnp.bfloat16)

def reference(latents, noise, timesteps, reward_dir, gain, time_scale, w_in, w_out):
    image_count = N_DP * MICRO
    latent_blocks = latents.reshape(image_count, ROWS_MB, C)
    noise_blocks = noise.reshape(image_count, ROWS_MB, C)
    loss_scale = 1.0 / math.sqrt(N_DP * MICRO * ROWS_MB)

    def per_image(grad_total, item):
        latent, noise_block, timestep = item
        embed = time_embed(timestep, C)
        hidden = latent
        inputs = []
        for section in range(N_SEGMENT):
            inputs.append(hidden)
            hidden = block_forward(hidden, gain[section], time_scale[section] * embed, w_in[section], w_out[section])[0]
        cotangent = sample_head(hidden, latent, noise_block, timestep, reward_dir, loss_scale)
        terms = [None] * N_SEGMENT
        for section in range(N_SEGMENT - 1, -1, -1):
            _, normed, preact, activation = block_forward(inputs[section], gain[section], time_scale[section] * embed, w_in[section], w_out[section])
            new_cot, grad_pre = block_backward(inputs[section], gain[section], preact, cotangent, w_in[section], w_out[section])
            terms[section] = weight_term(normed, grad_pre, activation, cotangent)
            cotangent = new_cot
        return (grad_total + jnp.stack(terms), None)
    grad_total, _ = lax.scan(per_image, jnp.zeros((N_SEGMENT, C, 2 * C), jnp.float32), (latent_blocks, noise_blocks, timesteps))
    return grad_total
```

```python
import functools
import math

import jax
import jax.numpy as jnp
from jax import lax
from jax.experimental import pallas as pl
from jax.experimental.pallas import tpu as pltpu
from jax.sharding import PartitionSpec as P

GROUPS = 32
NSTEPS = 1000
STRIDE = 20


EPS = 1e-05


def passed_along(shard, axis, by):
    length = lax.axis_size(axis)
    pairs = [(i, i + by) for i in range(length) if 0 <= i + by < length]
    return lax.ppermute(shard, axis, pairs)


def group_norm(state_f32, group_count):
    channels = state_f32.shape[1]
    per_group = channels // group_count
    col_mean = jnp.mean(state_f32, axis=0)
    group_mean = jnp.repeat(jnp.mean(col_mean.reshape(group_count, per_group), axis=1), per_group)
    centered = state_f32 - group_mean
    sq_mean = jnp.mean(centered * centered, axis=0)
    variance = jnp.repeat(jnp.mean(sq_mean.reshape(group_count, per_group), axis=1), per_group)
    return centered * lax.rsqrt(variance + EPS)


def time_embed(timestep, channels):
    half_width = channels // 2
    frequencies = jnp.exp(
        -math.log(10000.0) * jnp.arange(half_width).astype(jnp.float32) / half_width
    )
    phases = timestep.astype(jnp.float32) * frequencies
    return jnp.concatenate([jnp.sin(phases), jnp.cos(phases)])


def alpha_bar(timestep):
    value = ((timestep.astype(jnp.float32) + 1.0) / NSTEPS + 0.008) / 1.008 * (math.pi / 2.0)
    return jnp.cos(value) ** 2


def contract_rows(left, right):
    return lax.dot_general(
        left, right, (((0,), (0,)), ((), ())), preferred_element_type=jnp.float32
    )


def contract_cols(left, right):
    return lax.dot_general(
        left, right, (((1,), (1,)), ((), ())), preferred_element_type=jnp.float32
    )


def block_forward(hidden, gain_row, temb, first, second):
    state_f32 = hidden.astype(jnp.float32)
    normed = (group_norm(state_f32, GROUPS) * gain_row).astype(jnp.bfloat16)
    preact = jnp.dot(normed, first, preferred_element_type=jnp.float32) + temb
    activation = jax.nn.silu(preact).astype(jnp.bfloat16)
    result = (state_f32 + jnp.dot(activation, second, preferred_element_type=jnp.float32)).astype(
        jnp.bfloat16
    )
    return (result, normed, preact, activation)


def block_backward(hidden, gain_row, preact, cotangent, first, second):
    grad_act = contract_cols(cotangent, second)
    gate_value = jax.nn.sigmoid(preact)
    grad_pre = (grad_act * gate_value * (1.0 + preact * (1.0 - gate_value))).astype(jnp.bfloat16)
    grad_norm = contract_cols(grad_pre, first)
    _, pullback = jax.vjp(lambda values: group_norm(values, GROUPS), hidden.astype(jnp.float32))
    new_cot = (cotangent.astype(jnp.float32) + pullback(grad_norm * gain_row)[0]).astype(
        jnp.bfloat16
    )
    return (new_cot, grad_pre)


def weight_term(normed, grad_pre, activation, cotangent):
    return jnp.concatenate(
        [contract_rows(normed, grad_pre), contract_rows(activation, cotangent)], axis=1
    )


def sample_head(hidden, latent, noise_block, timestep, reward_dir, loss_scale):
    ab_now = alpha_bar(timestep)
    ab_prev = alpha_bar(timestep - STRIDE)
    coef_a = jnp.sqrt(ab_now)
    coef_b = jnp.sqrt(1.0 - ab_now)
    coef_p = jnp.sqrt(ab_prev)
    coef_q = jnp.sqrt(0.75 * (1.0 - ab_prev))
    coef_r = 0.5 * jnp.sqrt(1.0 - ab_prev)
    noise_pred, pullback = jax.vjp(
        lambda values: group_norm(values, GROUPS), hidden.astype(jnp.float32)
    )
    current = latent.astype(jnp.float32)
    previous = (
        coef_p * (current - coef_b * noise_pred) / coef_a
        + coef_q * noise_pred
        + coef_r * noise_block.astype(jnp.float32)
    )
    squashed = jnp.tanh(previous)
    grad_pred = (
        (coef_q - coef_p * coef_b / coef_a) * reward_dir * (1.0 - squashed * squashed) * loss_scale
    )
    return pullback(grad_pred)[0].astype(jnp.bfloat16)


def put_slot(buffer, value, slot_index):
    return lax.dynamic_update_index_in_dim(buffer, value, slot_index, 0)


def body(latents, noise, timesteps, reward_dir, gain, time_scale, w_in, w_out):
    segments = lax.axis_size("segment")
    segment_index = lax.axis_index("segment")
    last_segment = segments - 1
    micro_count = timesteps.shape[0]
    crop_rows = latents.shape[0] // micro_count
    channels = latents.shape[1]
    loss_scale = 1.0 / math.sqrt(lax.axis_size("dp") * latents.shape[0])
    tick_count = micro_count + segments - 1
    whole_in, whole_out = (
        lax.all_gather(w_in, "dp", axis=1, tiled=True),
        lax.all_gather(w_out, "dp", axis=1, tiled=True),
    )
    first = whole_in[0]
    second = whole_out[0]
    gain_row = gain[0]
    latent_blocks = latents.reshape(micro_count, crop_rows, channels)
    noise_blocks = noise.reshape(micro_count, crop_rows, channels)
    embeds = jax.vmap(lambda values: time_embed(values, channels))(timesteps) * time_scale[0]
    blank = jnp.zeros((crop_rows, channels), jnp.bfloat16)
    blank_stack = jnp.zeros((micro_count, crop_rows, channels), jnp.bfloat16)
    stored = ()

    def forward_tick(tick_index, state_carry):
        incoming, inputs, head_cots, kept = state_carry
        micro_index = tick_index - segment_index
        active = (micro_index >= 0) & (micro_index < micro_count)
        slot_index = jnp.clip(micro_index, 0, micro_count - 1)
        fresh_input = latent_blocks[slot_index]
        hidden = jnp.where(segment_index == 0, fresh_input, incoming)

        def forward_compute(buffers):
            inputs, head_cots, kept = buffers
            result, normed, preact, activation = block_forward(
                hidden, gain_row, embeds[slot_index], first, second
            )
            inputs = put_slot(inputs, hidden, slot_index)
            head_cot = lax.cond(
                segment_index == last_segment,
                lambda: sample_head(
                    result,
                    fresh_input,
                    noise_blocks[slot_index],
                    timesteps[slot_index],
                    reward_dir,
                    loss_scale,
                ),
                lambda: blank,
            )
            head_cots = put_slot(head_cots, head_cot, slot_index)
            return (result, inputs, head_cots, kept)

        def forward_skipped(buffers):
            return (blank, buffers[0], buffers[1], buffers[2])

        result, inputs, head_cots, kept = lax.cond(
            active, forward_compute, forward_skipped, (inputs, head_cots, kept)
        )
        incoming = passed_along(result, "segment", 1)
        return (incoming, inputs, head_cots, kept)

    _, inputs, head_cots, kept = lax.fori_loop(
        0, tick_count, forward_tick, (blank, blank_stack, blank_stack, stored)
    )
    grad_start = ()
    records = (blank_stack, blank_stack, blank_stack, blank_stack)

    def backward_tick(tick_index, state_carry):
        incoming, grad_sum, records = state_carry
        micro_index = tick_index - (last_segment - segment_index)
        active = (micro_index >= 0) & (micro_index < micro_count)
        slot_index = jnp.clip(micro_index, 0, micro_count - 1)
        cotangent = jnp.where(segment_index == last_segment, head_cots[slot_index], incoming)

        def backward_compute(buffers):
            grad_sum, records = buffers
            hidden = inputs[slot_index]
            _, normed, preact, activation = block_forward(
                hidden, gain_row, embeds[slot_index], first, second
            )
            new_cot, grad_pre = block_backward(hidden, gain_row, preact, cotangent, first, second)
            records = (
                put_slot(records[0], normed, slot_index),
                put_slot(records[1], grad_pre, slot_index),
                put_slot(records[2], activation, slot_index),
                put_slot(records[3], cotangent, slot_index),
            )
            return (new_cot, grad_sum, records)

        def backward_skipped(buffers):
            return (blank, buffers[0], buffers[1])

        result, grad_sum, records = lax.cond(
            active, backward_compute, backward_skipped, (grad_sum, records)
        )
        incoming = passed_along(result, "segment", -1)
        return (incoming, grad_sum, records)

    _, grad_sum, records = lax.fori_loop(0, tick_count, backward_tick, (blank, grad_start, records))
    flat = [buffer.reshape(micro_count * crop_rows, channels) for buffer in records]
    full_terms = weight_term(flat[0], flat[1], flat[2], flat[3])
    grad_rows = lax.psum_scatter(full_terms, "dp", scatter_dimension=0, tiled=True)
    return grad_rows[None]


def split_rows(values):
    high = values.astype(jnp.bfloat16).astype(jnp.float32)
    rest = values - high
    middle = rest.astype(jnp.bfloat16).astype(jnp.float32)
    low = rest - middle
    return jnp.concatenate([high, middle, low], axis=0).astype(jnp.bfloat16)


def step_kernel(
    shape,
    shard_ref,
    param_ref,
    latent_ref,
    noise_ref,
    embed_ref,
    reward_ref,
    coef_ref,
    out_ref,
    wbuf,
    pbuf,
    weights,
    states,
    normed,
    slopes,
    acts,
    cots,
    gradpre,
    means,
    scales,
    sums,
    spread,
    gather_mat,
    scatter_mat,
    grads,
    inbox0,
    inbox1,
    inbox2,
    inbox3,
    send_sem,
    recv_sem,
    local_sem,
):
    dp, depth, shard, channels, images, rows, loss_scale = shape
    me = lax.axis_index("dp")
    core = lax.axis_index("segment")
    other = 1 - core
    col = lax.rem(me, 4)
    z = me // 4
    qx = col + 1 - 2 * lax.rem(col, 2)
    qy = lax.rem(col + 2, 4)
    qd = 3 - col
    x_dev = (z * 4 + qx, core)
    y_dev = (z * 4 + qy, core)
    partner = (me, other)
    z_at = [lax.rem(z + dz, depth) for dz in range(depth)]
    z_from = [lax.rem(z + depth - dz, depth) for dz in range(depth)]
    z_dev = [(z_at[dz] * 4 + col, core) for dz in range(depth)]
    count = [0]
    pending = []

    def remote(src, dst, device):
        k = count[0]
        count[0] += 1
        copy = pltpu.make_async_remote_copy(
            src_ref=src,
            dst_ref=dst,
            send_sem=send_sem.at[k],
            recv_sem=recv_sem.at[k],
            device_id=device,
            device_id_type=pl.DeviceIdType.MESH,
        )
        copy.start()
        pending.append(copy)
        return copy

    barrier = pltpu.get_barrier_semaphore()
    friends = [x_dev, y_dev, partner] + z_dev[1:]
    for device in friends:
        pl.semaphore_signal(
            barrier, inc=1, device_id=device, device_id_type=pl.DeviceIdType.MESH
        )
    pl.semaphore_wait(barrier, len(friends))

    own = pltpu.make_async_copy(shard_ref, wbuf.at[core, col, z], local_sem.at[0])
    own.start()
    own_param = pltpu.make_async_copy(param_ref, pbuf.at[core], local_sem.at[1])
    own_param.start()

    to_z = [None] + [
        remote(shard_ref, wbuf.at[core, col, z], z_dev[dz]) for dz in range(1, depth)
    ]
    to_x = [remote(shard_ref, wbuf.at[core, col, z], x_dev)]
    to_y = [remote(shard_ref, wbuf.at[core, col, z], y_dev)]
    to_core = [
        remote(shard_ref, wbuf.at[core, col, z], partner),
        remote(param_ref, pbuf.at[core], partner),
    ]
    ch = lax.broadcasted_iota(jnp.int32, gather_mat.shape, 0)
    gr = lax.broadcasted_iota(jnp.int32, gather_mat.shape, 1) * (channels // GROUPS)
    inside = (ch >= gr) & (ch < gr + channels // GROUPS)
    gather_mat[...] = jnp.where(inside, 1.0, 0.0).astype(jnp.bfloat16)
    ch = lax.broadcasted_iota(jnp.int32, scatter_mat.shape, 1)
    gr = lax.broadcasted_iota(jnp.int32, scatter_mat.shape, 0) * (channels // GROUPS)
    inside = (ch >= gr) & (ch < gr + channels // GROUPS)
    scatter_mat[...] = jnp.where(inside, 1.0, 0.0).astype(jnp.bfloat16)
    sums[...] = jnp.zeros_like(sums)

    for dz in range(1, depth):
        to_z[dz].wait_recv()
        piece = wbuf.at[core, col, z_from[dz]]
        to_x.append(remote(piece, piece, x_dev))
        to_y.append(remote(piece, piece, y_dev))
        to_core.append(remote(piece, piece, partner))
    second = []
    for dz in range(depth):
        to_x[dz].wait_recv()
        to_y[dz].wait_recv()
        from_x = wbuf.at[core, qx, z_from[dz]]
        from_y = wbuf.at[core, qy, z_from[dz]]
        half_in, half_out = from_x.at[0], from_y.at[1]
        second.append(remote(half_in, half_in, y_dev))
        second.append(remote(half_out, half_out, x_dev))
        to_core.append(remote(from_x, from_x, partner))
        to_core.append(remote(from_y, from_y, partner))
    for dz in range(depth):
        second[2 * dz].wait_recv()
        second[2 * dz + 1].wait_recv()
        piece = wbuf.at[core, qd, z_from[dz]]
        to_core.append(remote(piece, piece, partner))
    own.wait()
    own_param.wait()
    for copy in to_core:
        copy.wait_recv()

    for section in range(2):
        for kind in range(2):
            for pair in range(dp // 2):
                q, zz = (2 * pair) % 4, pair // 2
                both = jnp.concatenate(
                    [
                        wbuf[section, q, zz, kind].astype(jnp.float32),
                        wbuf[section, q + 1, zz, kind].astype(jnp.float32),
                    ],
                    axis=0,
                )
                weights[section, kind, 2 * pair * shard : 2 * (pair + 1) * shard, :] = (
                    both.astype(jnp.bfloat16)
                )

    def group_means(values):
        parts = jnp.dot(
            split_rows(values), gather_mat[...], preferred_element_type=jnp.float32
        )
        lines = values.shape[0]
        total = parts[:lines] + parts[lines : 2 * lines] + parts[2 * lines :]
        total = total * (1.0 / (rows * (channels // GROUPS)))
        parts = jnp.dot(
            split_rows(total), scatter_mat[...], preferred_element_type=jnp.float32
        )
        return parts[:lines] + parts[lines : 2 * lines] + parts[2 * lines :]

    def statistics(stage):
        def mean_body(i, carry):
            block = states[stage, pl.ds(i * rows, rows), :].astype(jnp.float32)
            sums[pl.ds(i, 1), :] = jnp.sum(block, axis=0, keepdims=True)
            return carry

        lax.fori_loop(0, images, mean_body, 0)
        means[stage] = group_means(sums[...])

        def square_body(i, carry):
            block = states[stage, pl.ds(i * rows, rows), :].astype(jnp.float32)
            centered = block - means[stage, pl.ds(i, 1), :]
            sums[pl.ds(i, 1), :] = jnp.sum(centered * centered, axis=0, keepdims=True)
            return carry

        lax.fori_loop(0, images, square_body, 0)
        scales[stage] = lax.rsqrt(group_means(sums[...]) + EPS)

    def unit(stage, i):
        block = states[stage, pl.ds(i * rows, rows), :].astype(jnp.float32)
        return (block - means[stage, pl.ds(i, 1), :]) * scales[stage, pl.ds(i, 1), :]

    joint = 2 if images % 2 == 0 else 1
    base = core * (images * rows)

    def load_body(i, carry):
        where = pl.ds(pl.multiple_of(i * rows, rows), rows)
        states[0, where, :] = latent_ref[
            pl.ds(pl.multiple_of(base + i * rows, rows), rows), :
        ]
        return carry

    lax.fori_loop(0, images, load_body, 0)

    for section in range(2):
        statistics(section)
        gain_row = pbuf[section, 0:1, :]
        time_row = pbuf[section, 1:2, :]

        def forward_body(g, carry):
            for j in range(joint):
                i = g * joint + j
                where = pl.ds(pl.multiple_of(i * rows, rows), rows)
                normed[section, where, :] = (unit(section, i) * gain_row).astype(jnp.bfloat16)
            span = pl.ds(pl.multiple_of(g * joint * rows, rows), joint * rows)
            product = jnp.dot(
                normed[section, span, :],
                weights[section, 0],
                preferred_element_type=jnp.float32,
            )
            for j in range(joint):
                i = g * joint + j
                where = pl.ds(pl.multiple_of(i * rows, rows), rows)
                preact = product[j * rows : (j + 1) * rows] + time_row * embed_ref[pl.ds(i, 1), :]
                gate = jax.nn.sigmoid(preact)
                acts[section, where, :] = (preact * gate).astype(jnp.bfloat16)
                slopes[section, where, :] = gate * (1.0 + preact * (1.0 - gate))
            product = jnp.dot(
                acts[section, span, :],
                weights[section, 1],
                preferred_element_type=jnp.float32,
            )
            states[section + 1, span, :] = (
                states[section, span, :].astype(jnp.float32) + product
            ).astype(jnp.bfloat16)
            return carry

        lax.fori_loop(0, images // joint, forward_body, 0)

    statistics(2)

    def head_body(i, carry):
        where = pl.ds(pl.multiple_of(i * rows, rows), rows)
        pred = unit(2, i)
        current = states[0, where, :].astype(jnp.float32)
        fresh = noise_ref[pl.ds(pl.multiple_of(base + i * rows, rows), rows), :].astype(
            jnp.float32
        )
        keep, pull, stir = coef_ref[0, i], coef_ref[1, i], coef_ref[2, i]
        squashed = jnp.tanh(keep * current + pull * pred + stir * fresh)
        grad = (1.0 - squashed * squashed) * (reward_ref[...] * (pull * loss_scale))
        spread[where, :] = grad
        sums[pl.ds(i, 1), :] = jnp.sum(grad, axis=0, keepdims=True)
        sums[pl.ds(images + i, 1), :] = jnp.sum(grad * pred, axis=0, keepdims=True)
        return carry

    lax.fori_loop(0, images, head_body, 0)

    def pull_back(stage, incoming):
        means_two = group_means(sums[...])
        sums[...] = means_two

        def body(i, carry):
            where = pl.ds(pl.multiple_of(i * rows, rows), rows)
            pulled = scales[stage, pl.ds(i, 1), :] * (
                spread[where, :]
                - sums[pl.ds(i, 1), :]
                - unit(stage, i) * sums[pl.ds(images + i, 1), :]
            )
            if incoming is not None:
                pulled = cots[incoming, where, :].astype(jnp.float32) + pulled
            cots[stage - 1, where, :] = pulled.astype(jnp.bfloat16)
            return carry

        lax.fori_loop(0, images, body, 0)

    pull_back(2, None)

    for section in (1, 0):
        gain_row = pbuf[section, 0:1, :]

        def backward_body(g, carry):
            span = pl.ds(pl.multiple_of(g * joint * rows, rows), joint * rows)
            product = contract_cols(cots[section, span, :], weights[section, 1])
            gradpre[section, span, :] = (product * slopes[section, span, :]).astype(jnp.bfloat16)
            if section > 0:
                product = contract_cols(gradpre[section, span, :], weights[section, 0])
                for j in range(joint):
                    i = g * joint + j
                    where = pl.ds(pl.multiple_of(i * rows, rows), rows)
                    grad = product[j * rows : (j + 1) * rows] * gain_row
                    spread[where, :] = grad
                    sums[pl.ds(i, 1), :] = jnp.sum(grad, axis=0, keepdims=True)
                    sums[pl.ds(images + i, 1), :] = jnp.sum(
                        grad * unit(section, i), axis=0, keepdims=True
                    )
            return carry

        lax.fori_loop(0, images // joint, backward_body, 0)
        if section > 0:
            pull_back(section, section)
        for kind in range(2):
            if kind == 0:
                term = contract_rows(normed[section], gradpre[section])
            else:
                term = contract_rows(acts[section], cots[section])
            for owner in range(dp):
                grads[section, kind, owner % 4, owner // 4] = term[
                    owner * shard : (owner + 1) * shard
                ]

    def add(kind, q, values_ref):
        def body(k, carry):
            grads[core, kind, q, k] = grads[core, kind, q, k] + values_ref[k]
            return carry

        lax.fori_loop(0, depth, body, 0)

    order = ((qd, qd), (qx, qy), (qy, qx), (col, col))
    swaps = {}
    for step in range(4):
        for kind in range(2):
            q = order[step][kind]
            swaps[step, kind] = remote(
                grads.at[other, kind, q], inbox0.at[kind, q], partner
            )
    first = {}
    final = {}
    cross = ((x_dev, qx, qy), (y_dev, qy, qx))
    for step in range(2):
        for kind in range(2):
            q = order[step][kind]
            swaps[step, kind].wait_recv()
            add(kind, q, inbox0.at[kind, q])
            first[step, kind] = remote(
                grads.at[core, kind, q], inbox1.at[kind, step], cross[kind][0]
            )
    for kind in range(2):
        q = order[2][kind]
        swaps[2, kind].wait_recv()
        add(kind, q, inbox0.at[kind, q])
        first[0, kind].wait_recv()
        add(kind, q, inbox1.at[kind, 0])
        final[kind] = remote(grads.at[core, kind, q], inbox2.at[kind], cross[1 - kind][0])
    last = {}
    for kind in range(2):
        swaps[3, kind].wait_recv()
        add(kind, col, inbox0.at[kind, col])
        first[1, kind].wait_recv()
        add(kind, col, inbox1.at[kind, 1])
        final[kind].wait_recv()
        add(kind, col, inbox2.at[kind])
        for dz in range(1, depth):
            last[kind, dz] = remote(
                grads.at[core, kind, col, z_at[dz]], inbox3.at[kind, dz], z_dev[dz]
            )
    for kind in range(2):
        total = grads[core, kind, col, z]
        for dz in range(1, depth):
            last[kind, dz].wait_recv()
            total = total + inbox3[kind, dz]
        out_ref[:, kind * channels : (kind + 1) * channels] = total
    for copy in pending:
        copy.wait_send()


def fused_body(latents, noise, timesteps, reward_dir, gain, time_scale, w_in, w_out):
    dp = lax.axis_size("dp")
    depth = dp // 4
    core = lax.axis_index("segment")
    micro_count = timesteps.shape[0]
    images = micro_count // 2
    rows = latents.shape[0] // micro_count
    channels = latents.shape[1]
    shard = w_in.shape[1]
    loss_scale = 1.0 / math.sqrt(dp * latents.shape[0])
    times = lax.dynamic_slice_in_dim(timesteps, core * images, images)
    embeds = jax.vmap(lambda values: time_embed(values, channels))(times)
    ab_now, ab_prev = alpha_bar(times), alpha_bar(times - STRIDE)
    coef_a, coef_b = jnp.sqrt(ab_now), jnp.sqrt(1.0 - ab_now)
    coef_p, coef_q = jnp.sqrt(ab_prev), jnp.sqrt(0.75 * (1.0 - ab_prev))
    coefs = jnp.stack(
        [coef_p / coef_a, coef_q - coef_p * coef_b / coef_a, 0.5 * jnp.sqrt(1.0 - ab_prev)]
    )
    shards = jnp.concatenate([w_in, w_out], axis=0)
    params = jnp.concatenate([gain, time_scale, jnp.zeros((6, channels), jnp.float32)], axis=0)
    shape = (dp, depth, shard, channels, images, rows, loss_scale)
    total_rows = images * rows
    bf16, f32 = jnp.bfloat16, jnp.float32
    lines = -(-2 * images // 8) * 8
    square = (shard, channels)
    copies = 96 * depth
    vmem = pl.BlockSpec(memory_space=pltpu.VMEM)
    grad_rows = pl.pallas_call(
        functools.partial(step_kernel, shape),
        out_shape=jax.ShapeDtypeStruct((shard, 2 * channels), f32),
        in_specs=[vmem] * 6 + [pl.BlockSpec(memory_space=pltpu.SMEM)],
        out_specs=vmem,
        scratch_shapes=[
            pltpu.VMEM((2, 4, depth, 2) + square, bf16),
            pltpu.VMEM((2, 8, channels), f32),
            pltpu.VMEM((2, 2, channels, channels), bf16),
            pltpu.VMEM((3, total_rows, channels), bf16),
            pltpu.VMEM((2, total_rows, channels), bf16),
            pltpu.VMEM((2, total_rows, channels), f32),
            pltpu.VMEM((2, total_rows, channels), bf16),
            pltpu.VMEM((2, total_rows, channels), bf16),
            pltpu.VMEM((2, total_rows, channels), bf16),
            pltpu.VMEM((3, lines, channels), f32),
            pltpu.VMEM((3, lines, channels), f32),
            pltpu.VMEM((lines, channels), f32),
            pltpu.VMEM((total_rows, channels), f32),
            pltpu.VMEM((channels, 128), bf16),
            pltpu.VMEM((128, channels), bf16),
            pltpu.VMEM((2, 2, 4, depth) + square, f32),
            pltpu.VMEM((2, 4, depth) + square, f32),
            pltpu.VMEM((2, 2, depth) + square, f32),
            pltpu.VMEM((2, depth) + square, f32),
            pltpu.VMEM((2, depth) + square, f32),
            pltpu.SemaphoreType.DMA((copies,)),
            pltpu.SemaphoreType.DMA((copies,)),
            pltpu.SemaphoreType.DMA((2,)),
        ],
        compiler_params=pltpu.CompilerParams(
            collective_id=0, has_side_effects=True, vmem_limit_bytes=60 * 1024 * 1024
        ),
    )(shards, params, latents, noise, embeds, reward_dir[None], coefs)
    return grad_rows[None]


def fits(mesh):
    return mesh.shape["segment"] == 2 and mesh.shape["dp"] % 4 == 0


def solution(mesh):
    placed = (
        P("dp", None),
        P("dp", None),
        P("dp"),
        P(),
        P("segment", None),
        P("segment", None),
        P("segment", "dp", None),
        P("segment", "dp", None),
    )
    return jax.shard_map(
        fused_body if fits(mesh) else body, mesh=mesh, in_specs=placed, out_specs=P("segment", "dp", None), check_vma=False
    )
```

```python
import functools
import math

import jax
import jax.numpy as jnp
from jax import lax
from jax.experimental import pallas as pl
from jax.experimental.pallas import tpu as pltpu
from jax.sharding import PartitionSpec as P

GROUPS = 32
NSTEPS = 1000
STRIDE = 20


EPS = 1e-05


def passed_along(shard, axis, by):
    length = lax.axis_size(axis)
    pairs = [(i, i + by) for i in range(length) if 0 <= i + by < length]
    return lax.ppermute(shard, axis, pairs)


def group_norm(state_f32, group_count):
    channels = state_f32.shape[1]
    per_group = channels // group_count
    col_mean = jnp.mean(state_f32, axis=0)
    group_mean = jnp.repeat(jnp.mean(col_mean.reshape(group_count, per_group), axis=1), per_group)
    centered = state_f32 - group_mean
    sq_mean = jnp.mean(centered * centered, axis=0)
    variance = jnp.repeat(jnp.mean(sq_mean.reshape(group_count, per_group), axis=1), per_group)
    return centered * lax.rsqrt(variance + EPS)


def time_embed(timestep, channels):
    half_width = channels // 2
    frequencies = jnp.exp(
        -math.log(10000.0) * jnp.arange(half_width).astype(jnp.float32) / half_width
    )
    phases = timestep.astype(jnp.float32) * frequencies
    return jnp.concatenate([jnp.sin(phases), jnp.cos(phases)])


def alpha_bar(timestep):
    value = ((timestep.astype(jnp.float32) + 1.0) / NSTEPS + 0.008) / 1.008 * (math.pi / 2.0)
    return jnp.cos(value) ** 2


def contract_rows(left, right):
    return lax.dot_general(
        left, right, (((0,), (0,)), ((), ())), preferred_element_type=jnp.float32
    )


def contract_cols(left, right):
    return lax.dot_general(
        left, right, (((1,), (1,)), ((), ())), preferred_element_type=jnp.float32
    )


def block_forward(hidden, gain_row, temb, first, second):
    state_f32 = hidden.astype(jnp.float32)
    normed = (group_norm(state_f32, GROUPS) * gain_row).astype(jnp.bfloat16)
    preact = jnp.dot(normed, first, preferred_element_type=jnp.float32) + temb
    activation = jax.nn.silu(preact).astype(jnp.bfloat16)
    result = (state_f32 + jnp.dot(activation, second, preferred_element_type=jnp.float32)).astype(
        jnp.bfloat16
    )
    return (result, normed, preact, activation)


def block_backward(hidden, gain_row, preact, cotangent, first, second):
    grad_act = contract_cols(cotangent, second)
    gate_value = jax.nn.sigmoid(preact)
    grad_pre = (grad_act * gate_value * (1.0 + preact * (1.0 - gate_value))).astype(jnp.bfloat16)
    grad_norm = contract_cols(grad_pre, first)
    _, pullback = jax.vjp(lambda values: group_norm(values, GROUPS), hidden.astype(jnp.float32))
    new_cot = (cotangent.astype(jnp.float32) + pullback(grad_norm * gain_row)[0]).astype(
        jnp.bfloat16
    )
    return (new_cot, grad_pre)


def weight_term(normed, grad_pre, activation, cotangent):
    return jnp.concatenate(
        [contract_rows(normed, grad_pre), contract_rows(activation, cotangent)], axis=1
    )


def sample_head(hidden, latent, noise_block, timestep, reward_dir, loss_scale):
    ab_now = alpha_bar(timestep)
    ab_prev = alpha_bar(timestep - STRIDE)
    coef_a = jnp.sqrt(ab_now)
    coef_b = jnp.sqrt(1.0 - ab_now)
    coef_p = jnp.sqrt(ab_prev)
    coef_q = jnp.sqrt(0.75 * (1.0 - ab_prev))
    coef_r = 0.5 * jnp.sqrt(1.0 - ab_prev)
    noise_pred, pullback = jax.vjp(
        lambda values: group_norm(values, GROUPS), hidden.astype(jnp.float32)
    )
    current = latent.astype(jnp.float32)
    previous = (
        coef_p * (current - coef_b * noise_pred) / coef_a
        + coef_q * noise_pred
        + coef_r * noise_block.astype(jnp.float32)
    )
    squashed = jnp.tanh(previous)
    grad_pred = (
        (coef_q - coef_p * coef_b / coef_a) * reward_dir * (1.0 - squashed * squashed) * loss_scale
    )
    return pullback(grad_pred)[0].astype(jnp.bfloat16)


def put_slot(buffer, value, slot_index):
    return lax.dynamic_update_index_in_dim(buffer, value, slot_index, 0)


def body(latents, noise, timesteps, reward_dir, gain, time_scale, w_in, w_out):
    segments = lax.axis_size("segment")
    segment_index = lax.axis_index("segment")
    last_segment = segments - 1
    micro_count = timesteps.shape[0]
    crop_rows = latents.shape[0] // micro_count
    channels = latents.shape[1]
    loss_scale = 1.0 / math.sqrt(lax.axis_size("dp") * latents.shape[0])
    tick_count = micro_count + segments - 1
    whole_in, whole_out = (
        lax.all_gather(w_in, "dp", axis=1, tiled=True),
        lax.all_gather(w_out, "dp", axis=1, tiled=True),
    )
    first = whole_in[0]
    second = whole_out[0]
    gain_row = gain[0]
    latent_blocks = latents.reshape(micro_count, crop_rows, channels)
    noise_blocks = noise.reshape(micro_count, crop_rows, channels)
    embeds = jax.vmap(lambda values: time_embed(values, channels))(timesteps) * time_scale[0]
    blank = jnp.zeros((crop_rows, channels), jnp.bfloat16)
    blank_stack = jnp.zeros((micro_count, crop_rows, channels), jnp.bfloat16)
    stored = ()

    def forward_tick(tick_index, state_carry):
        incoming, inputs, head_cots, kept = state_carry
        micro_index = tick_index - segment_index
        active = (micro_index >= 0) & (micro_index < micro_count)
        slot_index = jnp.clip(micro_index, 0, micro_count - 1)
        fresh_input = latent_blocks[slot_index]
        hidden = jnp.where(segment_index == 0, fresh_input, incoming)

        def forward_compute(buffers):
            inputs, head_cots, kept = buffers
            result, normed, preact, activation = block_forward(
                hidden, gain_row, embeds[slot_index], first, second
            )
            inputs = put_slot(inputs, hidden, slot_index)
            head_cot = lax.cond(
                segment_index == last_segment,
                lambda: sample_head(
                    result,
                    fresh_input,
                    noise_blocks[slot_index],
                    timesteps[slot_index],
                    reward_dir,
                    loss_scale,
                ),
                lambda: blank,
            )
            head_cots = put_slot(head_cots, head_cot, slot_index)
            return (result, inputs, head_cots, kept)

        def forward_skipped(buffers):
            return (blank, buffers[0], buffers[1], buffers[2])

        result, inputs, head_cots, kept = lax.cond(
            active, forward_compute, forward_skipped, (inputs, head_cots, kept)
        )
        incoming = passed_along(result, "segment", 1)
        return (incoming, inputs, head_cots, kept)

    _, inputs, head_cots, kept = lax.fori_loop(
        0, tick_count, forward_tick, (blank, blank_stack, blank_stack, stored)
    )
    grad_start = ()
    records = (blank_stack, blank_stack, blank_stack, blank_stack)

    def backward_tick(tick_index, state_carry):
        incoming, grad_sum, records = state_carry
        micro_index = tick_index - (last_segment - segment_index)
        active = (micro_index >= 0) & (micro_index < micro_count)
        slot_index = jnp.clip(micro_index, 0, micro_count - 1)
        cotangent = jnp.where(segment_index == last_segment, head_cots[slot_index], incoming)

        def backward_compute(buffers):
            grad_sum, records = buffers
            hidden = inputs[slot_index]
            _, normed, preact, activation = block_forward(
                hidden, gain_row, embeds[slot_index], first, second
            )
            new_cot, grad_pre = block_backward(hidden, gain_row, preact, cotangent, first, second)
            records = (
                put_slot(records[0], normed, slot_index),
                put_slot(records[1], grad_pre, slot_index),
                put_slot(records[2], activation, slot_index),
                put_slot(records[3], cotangent, slot_index),
            )
            return (new_cot, grad_sum, records)

        def backward_skipped(buffers):
            return (blank, buffers[0], buffers[1])

        result, grad_sum, records = lax.cond(
            active, backward_compute, backward_skipped, (grad_sum, records)
        )
        incoming = passed_along(result, "segment", -1)
        return (incoming, grad_sum, records)

    _, grad_sum, records = lax.fori_loop(0, tick_count, backward_tick, (blank, grad_start, records))
    flat = [buffer.reshape(micro_count * crop_rows, channels) for buffer in records]
    full_terms = weight_term(flat[0], flat[1], flat[2], flat[3])
    grad_rows = lax.psum_scatter(full_terms, "dp", scatter_dimension=0, tiled=True)
    return grad_rows[None]


def split_rows(values):
    high = values.astype(jnp.bfloat16).astype(jnp.float32)
    rest = values - high
    middle = rest.astype(jnp.bfloat16).astype(jnp.float32)
    low = rest - middle
    return jnp.concatenate([high, middle, low], axis=0).astype(jnp.bfloat16)


class Pair:
    def __init__(self, copies):
        self.copies = copies

    def wait_recv(self):
        for copy in self.copies:
            copy.wait_recv()


def step_kernel(
    shape,
    win_ref,
    wout_ref,
    gain_ref,
    time_ref,
    latent_ref,
    noise_ref,
    embed_ref,
    reward_ref,
    coef_ref,
    out_ref,
    wbuf,
    pbuf,
    weights,
    states,
    noises,
    normed,
    slopes,
    acts,
    cots,
    gradpre,
    means,
    scales,
    sums,
    spread,
    gather_mat,
    scatter_mat,
    grads,
    inbox0,
    inbox1,
    inbox2,
    inbox3,
    send_sem,
    recv_sem,
    local_sem,
):
    dp, depth, shard, channels, images, rows, loss_scale = shape
    me = lax.axis_index("dp")
    core = lax.axis_index("segment")
    other = 1 - core
    col = lax.rem(me, 4)
    z = me // 4
    qx = col + 1 - 2 * lax.rem(col, 2)
    qy = lax.rem(col + 2, 4)
    qd = 3 - col
    x_dev = (z * 4 + qx, core)
    y_dev = (z * 4 + qy, core)
    partner = (me, other)
    z_at = [lax.rem(z + dz, depth) for dz in range(depth)]
    z_from = [lax.rem(z + depth - dz, depth) for dz in range(depth)]
    z_dev = [(z_at[dz] * 4 + col, core) for dz in range(depth)]
    count = [0]
    pending = []

    def remote(src, dst, device):
        k = count[0]
        count[0] += 1
        copy = pltpu.make_async_remote_copy(
            src_ref=src,
            dst_ref=dst,
            send_sem=send_sem.at[k],
            recv_sem=recv_sem.at[k],
            device_id=device,
            device_id_type=pl.DeviceIdType.MESH,
        )
        copy.start()
        pending.append(copy)
        return copy

    base = pl.multiple_of(core * (images * rows), images * rows)
    locals_ = [
        pltpu.make_async_copy(source, target, local_sem.at[k])
        for k, (source, target) in enumerate(
            (
                (win_ref.at[0], wbuf.at[core, col, z, 0]),
                (wout_ref.at[0], wbuf.at[core, col, z, 1]),
                (gain_ref, pbuf.at[core, 0]),
                (time_ref, pbuf.at[core, 1]),
                (latent_ref.at[pl.ds(base, images * rows)], states.at[0]),
                (noise_ref.at[pl.ds(base, images * rows)], noises),
            )
        )
    ]
    for copy in locals_:
        copy.start()

    barrier = pltpu.get_barrier_semaphore()
    friends = [x_dev, y_dev, partner] + z_dev[1:]
    for device in friends:
        pl.semaphore_signal(
            barrier, inc=1, device_id=device, device_id_type=pl.DeviceIdType.MESH
        )
    pl.semaphore_wait(barrier, len(friends))

    def own_shard(device):
        return Pair(
            [
                remote(source.at[0], wbuf.at[core, col, z, kind], device)
                for kind, source in enumerate((win_ref, wout_ref))
            ]
        )

    to_z = [None] + [own_shard(z_dev[dz]) for dz in range(1, depth)]
    to_x = [own_shard(x_dev)]
    to_y = [own_shard(y_dev)]
    to_core = [
        own_shard(partner),
        remote(gain_ref, pbuf.at[core, 0], partner),
        remote(time_ref, pbuf.at[core, 1], partner),
    ]
    ch = lax.broadcasted_iota(jnp.int32, gather_mat.shape, 0)
    gr = lax.broadcasted_iota(jnp.int32, gather_mat.shape, 1) * (channels // GROUPS)
    inside = (ch >= gr) & (ch < gr + channels // GROUPS)
    gather_mat[...] = jnp.where(inside, 1.0, 0.0).astype(jnp.bfloat16)
    ch = lax.broadcasted_iota(jnp.int32, scatter_mat.shape, 1)
    gr = lax.broadcasted_iota(jnp.int32, scatter_mat.shape, 0) * (channels // GROUPS)
    inside = (ch >= gr) & (ch < gr + channels // GROUPS)
    scatter_mat[...] = jnp.where(inside, 1.0, 0.0).astype(jnp.bfloat16)
    sums[...] = jnp.zeros_like(sums)

    for dz in range(1, depth):
        to_z[dz].wait_recv()
        piece = wbuf.at[core, col, z_from[dz]]
        to_x.append(remote(piece, piece, x_dev))
        to_y.append(remote(piece, piece, y_dev))
        to_core.append(remote(piece, piece, partner))
    second = []
    for dz in range(depth):
        to_x[dz].wait_recv()
        to_y[dz].wait_recv()
        from_x = wbuf.at[core, qx, z_from[dz]]
        from_y = wbuf.at[core, qy, z_from[dz]]
        half_in, half_out = from_x.at[0], from_y.at[1]
        second.append(remote(half_in, half_in, y_dev))
        second.append(remote(half_out, half_out, x_dev))
        to_core.append(remote(from_x, from_x, partner))
        to_core.append(remote(from_y, from_y, partner))
    for dz in range(depth):
        second[2 * dz].wait_recv()
        second[2 * dz + 1].wait_recv()
        piece = wbuf.at[core, qd, z_from[dz]]
        to_core.append(remote(piece, piece, partner))
    for copy in locals_:
        copy.wait()
    for copy in to_core:
        copy.wait_recv()

    for section in range(2):
        for kind in range(2):
            for pair in range(dp // 2):
                q, zz = (2 * pair) % 4, pair // 2
                both = jnp.concatenate(
                    [
                        wbuf[section, q, zz, kind].astype(jnp.float32),
                        wbuf[section, q + 1, zz, kind].astype(jnp.float32),
                    ],
                    axis=0,
                )
                weights[section, kind, 2 * pair * shard : 2 * (pair + 1) * shard, :] = (
                    both.astype(jnp.bfloat16)
                )

    def group_means(values):
        parts = jnp.dot(
            split_rows(values), gather_mat[...], preferred_element_type=jnp.float32
        )
        lines = values.shape[0]
        total = parts[:lines] + parts[lines : 2 * lines] + parts[2 * lines :]
        total = total * (1.0 / (rows * (channels // GROUPS)))
        parts = jnp.dot(
            split_rows(total), scatter_mat[...], preferred_element_type=jnp.float32
        )
        return parts[:lines] + parts[lines : 2 * lines] + parts[2 * lines :]

    def statistics(stage):
        def mean_body(i, carry):
            block = states[stage, pl.ds(i * rows, rows), :].astype(jnp.float32)
            sums[pl.ds(i, 1), :] = jnp.sum(block, axis=0, keepdims=True)
            return carry

        lax.fori_loop(0, images, mean_body, 0)
        means[stage] = group_means(sums[...])

        def square_body(i, carry):
            block = states[stage, pl.ds(i * rows, rows), :].astype(jnp.float32)
            centered = block - means[stage, pl.ds(i, 1), :]
            sums[pl.ds(i, 1), :] = jnp.sum(centered * centered, axis=0, keepdims=True)
            return carry

        lax.fori_loop(0, images, square_body, 0)
        scales[stage] = lax.rsqrt(group_means(sums[...]) + EPS)

    def unit(stage, i):
        block = states[stage, pl.ds(i * rows, rows), :].astype(jnp.float32)
        return (block - means[stage, pl.ds(i, 1), :]) * scales[stage, pl.ds(i, 1), :]

    joint = 2 if images % 2 == 0 else 1
    for section in range(2):
        statistics(section)
        gain_row = pbuf[section, 0]
        time_row = pbuf[section, 1]

        def forward_body(g, carry):
            for j in range(joint):
                i = g * joint + j
                where = pl.ds(pl.multiple_of(i * rows, rows), rows)
                normed[section, where, :] = (unit(section, i) * gain_row).astype(jnp.bfloat16)
            span = pl.ds(pl.multiple_of(g * joint * rows, rows), joint * rows)
            product = jnp.dot(
                normed[section, span, :],
                weights[section, 0],
                preferred_element_type=jnp.float32,
            )
            for j in range(joint):
                i = g * joint + j
                where = pl.ds(pl.multiple_of(i * rows, rows), rows)
                preact = product[j * rows : (j + 1) * rows] + time_row * embed_ref[pl.ds(i, 1), :]
                gate = jax.nn.sigmoid(preact)
                acts[section, where, :] = (preact * gate).astype(jnp.bfloat16)
                slopes[section, where, :] = gate * (1.0 + preact * (1.0 - gate))
            product = jnp.dot(
                acts[section, span, :],
                weights[section, 1],
                preferred_element_type=jnp.float32,
            )
            states[section + 1, span, :] = (
                states[section, span, :].astype(jnp.float32) + product
            ).astype(jnp.bfloat16)
            return carry

        lax.fori_loop(0, images // joint, forward_body, 0)

    statistics(2)

    def head_body(i, carry):
        where = pl.ds(pl.multiple_of(i * rows, rows), rows)
        pred = unit(2, i)
        current = states[0, where, :].astype(jnp.float32)
        fresh = noises[where, :].astype(jnp.float32)
        keep, pull, stir = coef_ref[0, i], coef_ref[1, i], coef_ref[2, i]
        squashed = jnp.tanh(keep * current + pull * pred + stir * fresh)
        grad = (1.0 - squashed * squashed) * (reward_ref[...][None] * (pull * loss_scale))
        spread[where, :] = grad
        sums[pl.ds(i, 1), :] = jnp.sum(grad, axis=0, keepdims=True)
        sums[pl.ds(images + i, 1), :] = jnp.sum(grad * pred, axis=0, keepdims=True)
        return carry

    lax.fori_loop(0, images, head_body, 0)

    def pull_back(stage, incoming):
        means_two = group_means(sums[...])
        sums[...] = means_two

        def body(i, carry):
            where = pl.ds(pl.multiple_of(i * rows, rows), rows)
            pulled = scales[stage, pl.ds(i, 1), :] * (
                spread[where, :]
                - sums[pl.ds(i, 1), :]
                - unit(stage, i) * sums[pl.ds(images + i, 1), :]
            )
            if incoming is not None:
                pulled = cots[incoming, where, :].astype(jnp.float32) + pulled
            cots[stage - 1, where, :] = pulled.astype(jnp.bfloat16)
            return carry

        lax.fori_loop(0, images, body, 0)

    pull_back(2, None)

    for section in (1, 0):
        gain_row = pbuf[section, 0]

        def backward_body(g, carry):
            span = pl.ds(pl.multiple_of(g * joint * rows, rows), joint * rows)
            product = contract_cols(cots[section, span, :], weights[section, 1])
            gradpre[section, span, :] = (product * slopes[section, span, :]).astype(jnp.bfloat16)
            if section > 0:
                product = contract_cols(gradpre[section, span, :], weights[section, 0])
                for j in range(joint):
                    i = g * joint + j
                    where = pl.ds(pl.multiple_of(i * rows, rows), rows)
                    grad = product[j * rows : (j + 1) * rows] * gain_row
                    spread[where, :] = grad
                    sums[pl.ds(i, 1), :] = jnp.sum(grad, axis=0, keepdims=True)
                    sums[pl.ds(images + i, 1), :] = jnp.sum(
                        grad * unit(section, i), axis=0, keepdims=True
                    )
            return carry

        lax.fori_loop(0, images // joint, backward_body, 0)
        if section > 0:
            pull_back(section, section)
        for kind in range(2):
            if kind == 0:
                term = contract_rows(normed[section], gradpre[section])
            else:
                term = contract_rows(acts[section], cots[section])
            for owner in range(dp):
                grads[section, kind, owner % 4, owner // 4] = term[
                    owner * shard : (owner + 1) * shard
                ]

    order = ((qd, qd), (qx, qy), (qy, qx), (col, col))
    cross = (x_dev, y_dev)
    chunks = [dz for dz in range(depth - 1, 0, -1)] + [0]
    kinds = range(2)
    swaps, first, final, last = {}, {}, {}, {}

    def mine(kind, q, dz):
        return grads.at[core, kind, q, z_at[dz]]

    def add(target, source):
        target[...] = target[...] + source[...]

    for dz in chunks:
        for step in range(4):
            for kind in kinds:
                q = order[step][kind]
                swaps[dz, step, kind] = remote(
                    grads.at[other, kind, q, z_at[dz]], inbox0.at[kind, q, z_at[dz]], partner
                )

    def summed(dz, step, kind):
        q = order[step][kind]
        swaps[dz, step, kind].wait_recv()
        add(mine(kind, q, dz), inbox0.at[kind, q, z_at[dz]])
        return mine(kind, q, dz)

    def stage_one(dz):
        for step in range(2):
            for kind in kinds:
                first[dz, step, kind] = remote(
                    summed(dz, step, kind), inbox1.at[kind, step, z_at[dz]], cross[kind]
                )

    def stage_two(dz):
        for kind in kinds:
            total = summed(dz, 2, kind)
            first[dz, 0, kind].wait_recv()
            add(total, inbox1.at[kind, 0, z_at[dz]])
            final[dz, kind] = remote(total, inbox2.at[kind, z_at[dz]], cross[1 - kind])

    def stage_three(dz):
        for kind in kinds:
            total = summed(dz, 3, kind)
            first[dz, 1, kind].wait_recv()
            add(total, inbox1.at[kind, 1, z_at[dz]])
            final[dz, kind].wait_recv()
            add(total, inbox2.at[kind, z_at[dz]])
            if dz > 0:
                last[dz, kind] = remote(total, inbox3.at[kind, dz], z_dev[dz])

    for turn in range(depth + 2):
        for lag, stage in ((0, stage_one), (1, stage_two), (2, stage_three)):
            if 0 <= turn - lag < depth:
                stage(chunks[turn - lag])
    for kind in kinds:
        total = mine(kind, col, 0)[...]
        for dz in chunks[:-1]:
            last[dz, kind].wait_recv()
            total = total + inbox3[kind, dz]
        out_ref[0, :, kind * channels : (kind + 1) * channels] = total
    for copy in pending:
        copy.wait_send()


def fused_body(latents, noise, timesteps, reward_dir, gain, time_scale, w_in, w_out):
    dp = lax.axis_size("dp")
    depth = dp // 4
    core = lax.axis_index("segment")
    micro_count = timesteps.shape[0]
    images = micro_count // 2
    rows = latents.shape[0] // micro_count
    channels = latents.shape[1]
    shard = w_in.shape[1]
    loss_scale = 1.0 / math.sqrt(dp * latents.shape[0])
    times = lax.dynamic_slice_in_dim(timesteps, core * images, images)
    embeds = jax.vmap(lambda values: time_embed(values, channels))(times)
    ab_now, ab_prev = alpha_bar(times), alpha_bar(times - STRIDE)
    coef_a, coef_b = jnp.sqrt(ab_now), jnp.sqrt(1.0 - ab_now)
    coef_p, coef_q = jnp.sqrt(ab_prev), jnp.sqrt(0.75 * (1.0 - ab_prev))
    coefs = jnp.stack(
        [coef_p / coef_a, coef_q - coef_p * coef_b / coef_a, 0.5 * jnp.sqrt(1.0 - ab_prev)]
    )
    shape = (dp, depth, shard, channels, images, rows, loss_scale)
    total_rows = images * rows
    bf16, f32 = jnp.bfloat16, jnp.float32
    lines = -(-2 * images // 8) * 8
    square = (shard, channels)
    copies = 64 * depth
    vmem = pl.BlockSpec(memory_space=pltpu.VMEM)
    grad_rows = pl.pallas_call(
        functools.partial(step_kernel, shape),
        out_shape=jax.ShapeDtypeStruct((1, shard, 2 * channels), f32),
        in_specs=[vmem] * 4 + [pl.BlockSpec(memory_space=pl.ANY)] * 2 + [vmem] * 2 + [pl.BlockSpec(memory_space=pltpu.SMEM)],
        out_specs=vmem,
        scratch_shapes=[
            pltpu.VMEM((2, 4, depth, 2) + square, bf16),
            pltpu.VMEM((2, 2, 1, channels), f32),
            pltpu.VMEM((2, 2, channels, channels), bf16),
            pltpu.VMEM((3, total_rows, channels), bf16),
            pltpu.VMEM((total_rows, channels), bf16),
            pltpu.VMEM((2, total_rows, channels), bf16),
            pltpu.VMEM((2, total_rows, channels), f32),
            pltpu.VMEM((2, total_rows, channels), bf16),
            pltpu.VMEM((2, total_rows, channels), bf16),
            pltpu.VMEM((2, total_rows, channels), bf16),
            pltpu.VMEM((3, lines, channels), f32),
            pltpu.VMEM((3, lines, channels), f32),
            pltpu.VMEM((lines, channels), f32),
            pltpu.VMEM((total_rows, channels), f32),
            pltpu.VMEM((channels, 128), bf16),
            pltpu.VMEM((128, channels), bf16),
            pltpu.VMEM((2, 2, 4, depth) + square, f32),
            pltpu.VMEM((2, 4, depth) + square, f32),
            pltpu.VMEM((2, 2, depth) + square, f32),
            pltpu.VMEM((2, depth) + square, f32),
            pltpu.VMEM((2, depth) + square, f32),
            pltpu.SemaphoreType.DMA((copies,)),
            pltpu.SemaphoreType.DMA((copies,)),
            pltpu.SemaphoreType.DMA((6,)),
        ],
        compiler_params=pltpu.CompilerParams(
            collective_id=0, has_side_effects=True, vmem_limit_bytes=60 * 1024 * 1024
        ),
    )(w_in, w_out, gain, time_scale, latents, noise, embeds, reward_dir, coefs)
    return grad_rows


def fits(mesh):
    return mesh.shape["segment"] == 2 and mesh.shape["dp"] % 4 == 0


def solution(mesh):
    placed = (
        P("dp", None),
        P("dp", None),
        P("dp"),
        P(),
        P("segment", None),
        P("segment", None),
        P("segment", "dp", None),
        P("segment", "dp", None),
    )
    return jax.shard_map(
        fused_body if fits(mesh) else body, mesh=mesh, in_specs=placed, out_specs=P("segment", "dp", None), check_vma=False
    )
```

```python
import functools
import math

import jax
import jax.numpy as jnp
from jax import lax
from jax.experimental import pallas as pl
from jax.experimental.pallas import tpu as pltpu
from jax.sharding import PartitionSpec as P

GROUPS = 32
NSTEPS = 1000
STRIDE = 20
LEAD = 2


EPS = 1e-05


def passed_along(shard, axis, by):
    length = lax.axis_size(axis)
    pairs = [(i, i + by) for i in range(length) if 0 <= i + by < length]
    return lax.ppermute(shard, axis, pairs)


def group_norm(state_f32, group_count):
    channels = state_f32.shape[1]
    per_group = channels // group_count
    col_mean = jnp.mean(state_f32, axis=0)
    group_mean = jnp.repeat(jnp.mean(col_mean.reshape(group_count, per_group), axis=1), per_group)
    centered = state_f32 - group_mean
    sq_mean = jnp.mean(centered * centered, axis=0)
    variance = jnp.repeat(jnp.mean(sq_mean.reshape(group_count, per_group), axis=1), per_group)
    return centered * lax.rsqrt(variance + EPS)


def time_embed(timestep, channels):
    half_width = channels // 2
    frequencies = jnp.exp(
        -math.log(10000.0) * jnp.arange(half_width).astype(jnp.float32) / half_width
    )
    phases = timestep.astype(jnp.float32) * frequencies
    return jnp.concatenate([jnp.sin(phases), jnp.cos(phases)])


def alpha_bar(timestep):
    value = ((timestep.astype(jnp.float32) + 1.0) / NSTEPS + 0.008) / 1.008 * (math.pi / 2.0)
    return jnp.cos(value) ** 2


def contract_rows(left, right):
    return lax.dot_general(
        left, right, (((0,), (0,)), ((), ())), preferred_element_type=jnp.float32
    )


def contract_cols(left, right):
    return lax.dot_general(
        left, right, (((1,), (1,)), ((), ())), preferred_element_type=jnp.float32
    )


def block_forward(hidden, gain_row, temb, first, second):
    state_f32 = hidden.astype(jnp.float32)
    normed = (group_norm(state_f32, GROUPS) * gain_row).astype(jnp.bfloat16)
    preact = jnp.dot(normed, first, preferred_element_type=jnp.float32) + temb
    activation = jax.nn.silu(preact).astype(jnp.bfloat16)
    result = (state_f32 + jnp.dot(activation, second, preferred_element_type=jnp.float32)).astype(
        jnp.bfloat16
    )
    return (result, normed, preact, activation)


def block_backward(hidden, gain_row, preact, cotangent, first, second):
    grad_act = contract_cols(cotangent, second)
    gate_value = jax.nn.sigmoid(preact)
    grad_pre = (grad_act * gate_value * (1.0 + preact * (1.0 - gate_value))).astype(jnp.bfloat16)
    grad_norm = contract_cols(grad_pre, first)
    _, pullback = jax.vjp(lambda values: group_norm(values, GROUPS), hidden.astype(jnp.float32))
    new_cot = (cotangent.astype(jnp.float32) + pullback(grad_norm * gain_row)[0]).astype(
        jnp.bfloat16
    )
    return (new_cot, grad_pre)


def weight_term(normed, grad_pre, activation, cotangent):
    return jnp.concatenate(
        [contract_rows(normed, grad_pre), contract_rows(activation, cotangent)], axis=1
    )


def sample_head(hidden, latent, noise_block, timestep, reward_dir, loss_scale):
    ab_now = alpha_bar(timestep)
    ab_prev = alpha_bar(timestep - STRIDE)
    coef_a = jnp.sqrt(ab_now)
    coef_b = jnp.sqrt(1.0 - ab_now)
    coef_p = jnp.sqrt(ab_prev)
    coef_q = jnp.sqrt(0.75 * (1.0 - ab_prev))
    coef_r = 0.5 * jnp.sqrt(1.0 - ab_prev)
    noise_pred, pullback = jax.vjp(
        lambda values: group_norm(values, GROUPS), hidden.astype(jnp.float32)
    )
    current = latent.astype(jnp.float32)
    previous = (
        coef_p * (current - coef_b * noise_pred) / coef_a
        + coef_q * noise_pred
        + coef_r * noise_block.astype(jnp.float32)
    )
    squashed = jnp.tanh(previous)
    grad_pred = (
        (coef_q - coef_p * coef_b / coef_a) * reward_dir * (1.0 - squashed * squashed) * loss_scale
    )
    return pullback(grad_pred)[0].astype(jnp.bfloat16)


def put_slot(buffer, value, slot_index):
    return lax.dynamic_update_index_in_dim(buffer, value, slot_index, 0)


def body(latents, noise, timesteps, reward_dir, gain, time_scale, w_in, w_out):
    segments = lax.axis_size("segment")
    segment_index = lax.axis_index("segment")
    last_segment = segments - 1
    micro_count = timesteps.shape[0]
    crop_rows = latents.shape[0] // micro_count
    channels = latents.shape[1]
    loss_scale = 1.0 / math.sqrt(lax.axis_size("dp") * latents.shape[0])
    tick_count = micro_count + segments - 1
    whole_in, whole_out = (
        lax.all_gather(w_in, "dp", axis=1, tiled=True),
        lax.all_gather(w_out, "dp", axis=1, tiled=True),
    )
    first = whole_in[0]
    second = whole_out[0]
    gain_row = gain[0]
    latent_blocks = latents.reshape(micro_count, crop_rows, channels)
    noise_blocks = noise.reshape(micro_count, crop_rows, channels)
    embeds = jax.vmap(lambda values: time_embed(values, channels))(timesteps) * time_scale[0]
    blank = jnp.zeros((crop_rows, channels), jnp.bfloat16)
    blank_stack = jnp.zeros((micro_count, crop_rows, channels), jnp.bfloat16)
    stored = ()

    def forward_tick(tick_index, state_carry):
        incoming, inputs, head_cots, kept = state_carry
        micro_index = tick_index - segment_index
        active = (micro_index >= 0) & (micro_index < micro_count)
        slot_index = jnp.clip(micro_index, 0, micro_count - 1)
        fresh_input = latent_blocks[slot_index]
        hidden = jnp.where(segment_index == 0, fresh_input, incoming)

        def forward_compute(buffers):
            inputs, head_cots, kept = buffers
            result, normed, preact, activation = block_forward(
                hidden, gain_row, embeds[slot_index], first, second
            )
            inputs = put_slot(inputs, hidden, slot_index)
            head_cot = lax.cond(
                segment_index == last_segment,
                lambda: sample_head(
                    result,
                    fresh_input,
                    noise_blocks[slot_index],
                    timesteps[slot_index],
                    reward_dir,
                    loss_scale,
                ),
                lambda: blank,
            )
            head_cots = put_slot(head_cots, head_cot, slot_index)
            return (result, inputs, head_cots, kept)

        def forward_skipped(buffers):
            return (blank, buffers[0], buffers[1], buffers[2])

        result, inputs, head_cots, kept = lax.cond(
            active, forward_compute, forward_skipped, (inputs, head_cots, kept)
        )
        incoming = passed_along(result, "segment", 1)
        return (incoming, inputs, head_cots, kept)

    _, inputs, head_cots, kept = lax.fori_loop(
        0, tick_count, forward_tick, (blank, blank_stack, blank_stack, stored)
    )
    grad_start = ()
    records = (blank_stack, blank_stack, blank_stack, blank_stack)

    def backward_tick(tick_index, state_carry):
        incoming, grad_sum, records = state_carry
        micro_index = tick_index - (last_segment - segment_index)
        active = (micro_index >= 0) & (micro_index < micro_count)
        slot_index = jnp.clip(micro_index, 0, micro_count - 1)
        cotangent = jnp.where(segment_index == last_segment, head_cots[slot_index], incoming)

        def backward_compute(buffers):
            grad_sum, records = buffers
            hidden = inputs[slot_index]
            _, normed, preact, activation = block_forward(
                hidden, gain_row, embeds[slot_index], first, second
            )
            new_cot, grad_pre = block_backward(hidden, gain_row, preact, cotangent, first, second)
            records = (
                put_slot(records[0], normed, slot_index),
                put_slot(records[1], grad_pre, slot_index),
                put_slot(records[2], activation, slot_index),
                put_slot(records[3], cotangent, slot_index),
            )
            return (new_cot, grad_sum, records)

        def backward_skipped(buffers):
            return (blank, buffers[0], buffers[1])

        result, grad_sum, records = lax.cond(
            active, backward_compute, backward_skipped, (grad_sum, records)
        )
        incoming = passed_along(result, "segment", -1)
        return (incoming, grad_sum, records)

    _, grad_sum, records = lax.fori_loop(0, tick_count, backward_tick, (blank, grad_start, records))
    flat = [buffer.reshape(micro_count * crop_rows, channels) for buffer in records]
    full_terms = weight_term(flat[0], flat[1], flat[2], flat[3])
    grad_rows = lax.psum_scatter(full_terms, "dp", scatter_dimension=0, tiled=True)
    return grad_rows[None]


def split_rows(values):
    high = values.astype(jnp.bfloat16).astype(jnp.float32)
    rest = values - high
    middle = rest.astype(jnp.bfloat16).astype(jnp.float32)
    low = rest - middle
    return jnp.concatenate([high, middle, low], axis=0).astype(jnp.bfloat16)


class Pair:
    def __init__(self, copies):
        self.copies = copies

    def wait_recv(self):
        for copy in self.copies:
            copy.wait_recv()


def step_kernel(
    shape,
    win_ref,
    wout_ref,
    gain_ref,
    time_ref,
    latent_ref,
    noise_ref,
    times_ref,
    reward_ref,
    out_ref,
    embed_ref,
    coef_ref,
    wbuf,
    pbuf,
    weights,
    states,
    noises,
    normed,
    slopes,
    acts,
    cots,
    gradpre,
    means,
    scales,
    sums,
    spread,
    gather_mat,
    scatter_mat,
    grads,
    inbox0,
    inbox1,
    inbox2,
    inbox3,
    result,
    closed,
    send_sem,
    recv_sem,
    local_sem,
):
    dp, depth, shard, channels, images, rows, loss_scale = shape
    me = lax.axis_index("dp")
    core = lax.axis_index("segment")
    other = 1 - core
    col = lax.rem(me, 4)
    z = me // 4
    qx = col + 1 - 2 * lax.rem(col, 2)
    qy = lax.rem(col + 2, 4)
    qd = 3 - col
    x_dev = (z * 4 + qx, core)
    y_dev = (z * 4 + qy, core)
    partner = (me, other)
    z_at = [lax.rem(z + dz, depth) for dz in range(depth)]
    z_from = [lax.rem(z + depth - dz, depth) for dz in range(depth)]
    z_dev = [(z_at[dz] * 4 + col, core) for dz in range(depth)]
    near = sorted(range(1, depth), key=lambda dz: (min(dz, depth - dz), dz))
    count = [0]
    pending = []

    def remote(src, dst, device):
        k = count[0]
        count[0] += 1
        copy = pltpu.make_async_remote_copy(
            src_ref=src,
            dst_ref=dst,
            send_sem=send_sem.at[k],
            recv_sem=recv_sem.at[k],
            device_id=device,
            device_id_type=pl.DeviceIdType.MESH,
        )
        copy.start()
        pending.append(copy)
        return copy

    base = pl.multiple_of(core * (images * rows), images * rows)
    locals_ = [
        pltpu.make_async_copy(source, target, local_sem.at[k])
        for k, (source, target) in enumerate(
            (
                (win_ref.at[0], wbuf.at[core, col, z, 0]),
                (wout_ref.at[0], wbuf.at[core, col, z, 1]),
                (gain_ref, pbuf.at[core, 0]),
                (time_ref, pbuf.at[core, 1]),
                (latent_ref.at[pl.ds(base, images * rows)], states.at[0]),
                (noise_ref.at[pl.ds(base, images * rows)], noises),
            )
        )
    ]
    for copy in locals_:
        copy.start()

    barrier = pltpu.get_barrier_semaphore()
    friends = [x_dev, y_dev, partner] + z_dev[1:]
    for device in friends:
        pl.semaphore_signal(
            barrier, inc=1, device_id=device, device_id_type=pl.DeviceIdType.MESH
        )
    pl.semaphore_wait(barrier, len(friends))

    def own_shard(device):
        return Pair(
            [
                remote(source.at[0], wbuf.at[core, col, z, kind], device)
                for kind, source in enumerate((win_ref, wout_ref))
            ]
        )

    to_x = [own_shard(x_dev)]
    to_y = [own_shard(y_dev)]
    to_z = {dz: own_shard(z_dev[dz]) for dz in near}
    to_core = [
        own_shard(partner),
        remote(gain_ref, pbuf.at[core, 0], partner),
        remote(time_ref, pbuf.at[core, 1], partner),
    ]
    ch = lax.broadcasted_iota(jnp.int32, gather_mat.shape, 0)
    gr = lax.broadcasted_iota(jnp.int32, gather_mat.shape, 1) * (channels // GROUPS)
    inside = (ch >= gr) & (ch < gr + channels // GROUPS)
    gather_mat[...] = jnp.where(inside, 1.0, 0.0).astype(jnp.bfloat16)
    ch = lax.broadcasted_iota(jnp.int32, scatter_mat.shape, 1)
    gr = lax.broadcasted_iota(jnp.int32, scatter_mat.shape, 0) * (channels // GROUPS)
    inside = (ch >= gr) & (ch < gr + channels // GROUPS)
    scatter_mat[...] = jnp.where(inside, 1.0, 0.0).astype(jnp.bfloat16)
    sums[...] = jnp.zeros_like(sums)

    def column(stacked):
        line = lax.broadcasted_iota(jnp.int32, stacked.shape, 0)
        values = jnp.zeros(stacked.shape, jnp.float32)
        for i in range(images):
            values = jnp.where(
                line == i, times_ref[core * images + i].astype(jnp.float32), values
            )
        return values

    half_width = channels // 2
    lane = lax.broadcasted_iota(jnp.int32, embed_ref.shape, 1)
    k_index = jnp.where(lane < half_width, lane, lane - half_width).astype(jnp.float32)
    phases = column(embed_ref) * jnp.exp(-math.log(10000.0) * k_index / half_width)
    embed_ref[...] = jnp.where(lane < half_width, jnp.sin(phases), jnp.cos(phases))
    now = column(coef_ref.at[0])
    ab_now, ab_prev = alpha_bar(now), alpha_bar(now - STRIDE)
    coef_a, coef_b = jnp.sqrt(ab_now), jnp.sqrt(1.0 - ab_now)
    coef_p, coef_q = jnp.sqrt(ab_prev), jnp.sqrt(0.75 * (1.0 - ab_prev))
    coef_ref[0] = coef_p / coef_a
    coef_ref[1] = coef_q - coef_p * coef_b / coef_a
    coef_ref[2] = 0.5 * jnp.sqrt(1.0 - ab_prev)

    for dz in near:
        to_z[dz].wait_recv()
        piece = wbuf.at[core, col, z_from[dz]]
        to_x.append(remote(piece, piece, x_dev))
        to_y.append(remote(piece, piece, y_dev))
        to_core.append(remote(piece, piece, partner))
    second = []
    for turn, dz in enumerate([0] + near):
        to_x[turn].wait_recv()
        to_y[turn].wait_recv()
        from_x = wbuf.at[core, qx, z_from[dz]]
        from_y = wbuf.at[core, qy, z_from[dz]]
        half_in, half_out = from_x.at[0], from_y.at[1]
        second.append(remote(half_in, half_in, y_dev))
        second.append(remote(half_out, half_out, x_dev))
        to_core.append(remote(from_x, from_x, partner))
        to_core.append(remote(from_y, from_y, partner))
    for turn, dz in enumerate([0] + near):
        second[2 * turn].wait_recv()
        second[2 * turn + 1].wait_recv()
        piece = wbuf.at[core, qd, z_from[dz]]
        to_core.append(remote(piece, piece, partner))
    for copy in locals_:
        copy.wait()
    for copy in to_core:
        copy.wait_recv()

    for section in range(2):
        for kind in range(2):
            for pair in range(dp // 2):
                q, zz = (2 * pair) % 4, pair // 2
                both = jnp.concatenate(
                    [
                        wbuf[section, q, zz, kind].astype(jnp.float32),
                        wbuf[section, q + 1, zz, kind].astype(jnp.float32),
                    ],
                    axis=0,
                )
                weights[section, kind, 2 * pair * shard : 2 * (pair + 1) * shard, :] = (
                    both.astype(jnp.bfloat16)
                )

    def group_means(values):
        parts = jnp.dot(
            split_rows(values), gather_mat[...], preferred_element_type=jnp.float32
        )
        lines = values.shape[0]
        total = parts[:lines] + parts[lines : 2 * lines] + parts[2 * lines :]
        total = total * (1.0 / (rows * (channels // GROUPS)))
        parts = jnp.dot(
            split_rows(total), scatter_mat[...], preferred_element_type=jnp.float32
        )
        return parts[:lines] + parts[lines : 2 * lines] + parts[2 * lines :]

    def statistics(stage):
        def mean_body(i, carry):
            block = states[stage, pl.ds(i * rows, rows), :].astype(jnp.float32)
            sums[pl.ds(i, 1), :] = jnp.sum(block, axis=0, keepdims=True)
            return carry

        lax.fori_loop(0, images, mean_body, 0)
        means[stage] = group_means(sums[...])

        def square_body(i, carry):
            block = states[stage, pl.ds(i * rows, rows), :].astype(jnp.float32)
            centered = block - means[stage, pl.ds(i, 1), :]
            sums[pl.ds(i, 1), :] = jnp.sum(centered * centered, axis=0, keepdims=True)
            return carry

        lax.fori_loop(0, images, square_body, 0)
        scales[stage] = lax.rsqrt(group_means(sums[...]) + EPS)

    def unit(stage, i):
        block = states[stage, pl.ds(i * rows, rows), :].astype(jnp.float32)
        return (block - means[stage, pl.ds(i, 1), :]) * scales[stage, pl.ds(i, 1), :]

    joint = 2 if images % 2 == 0 else 1
    for section in range(2):
        statistics(section)
        gain_row = pbuf[section, 0]
        time_row = pbuf[section, 1]

        def forward_body(g, carry):
            for j in range(joint):
                i = g * joint + j
                where = pl.ds(pl.multiple_of(i * rows, rows), rows)
                normed[section, where, :] = (unit(section, i) * gain_row).astype(jnp.bfloat16)
            span = pl.ds(pl.multiple_of(g * joint * rows, rows), joint * rows)
            product = jnp.dot(
                normed[section, span, :],
                weights[section, 0],
                preferred_element_type=jnp.float32,
            )
            for j in range(joint):
                i = g * joint + j
                where = pl.ds(pl.multiple_of(i * rows, rows), rows)
                preact = product[j * rows : (j + 1) * rows] + time_row * embed_ref[pl.ds(i, 1), :]
                gate = jax.nn.sigmoid(preact)
                acts[section, where, :] = (preact * gate).astype(jnp.bfloat16)
                slopes[section, where, :] = gate * (1.0 + preact * (1.0 - gate))
            product = jnp.dot(
                acts[section, span, :],
                weights[section, 1],
                preferred_element_type=jnp.float32,
            )
            states[section + 1, span, :] = (
                states[section, span, :].astype(jnp.float32) + product
            ).astype(jnp.bfloat16)
            return carry

        lax.fori_loop(0, images // joint, forward_body, 0)

    statistics(2)

    def head_body(i, carry):
        where = pl.ds(pl.multiple_of(i * rows, rows), rows)
        pred = unit(2, i)
        current = states[0, where, :].astype(jnp.float32)
        fresh = noises[where, :].astype(jnp.float32)
        keep, pull, stir = (coef_ref[j, pl.ds(i, 1), 0:1] for j in range(3))
        squashed = jnp.tanh(keep * current + pull * pred + stir * fresh)
        grad = (1.0 - squashed * squashed) * (reward_ref[...][None] * (pull * loss_scale))
        spread[where, :] = grad
        sums[pl.ds(i, 1), :] = jnp.sum(grad, axis=0, keepdims=True)
        sums[pl.ds(images + i, 1), :] = jnp.sum(grad * pred, axis=0, keepdims=True)
        return carry

    lax.fori_loop(0, images, head_body, 0)

    def pull_back(stage, incoming):
        means_two = group_means(sums[...])
        sums[...] = means_two

        def body(i, carry):
            where = pl.ds(pl.multiple_of(i * rows, rows), rows)
            pulled = scales[stage, pl.ds(i, 1), :] * (
                spread[where, :]
                - sums[pl.ds(i, 1), :]
                - unit(stage, i) * sums[pl.ds(images + i, 1), :]
            )
            if incoming is not None:
                pulled = cots[incoming, where, :].astype(jnp.float32) + pulled
            cots[stage - 1, where, :] = pulled.astype(jnp.bfloat16)
            return carry

        lax.fori_loop(0, images, body, 0)

    pull_back(2, None)

    qa = qx + core * (qy - qx)
    qb = qy + core * (qx - qy)
    a_dev, b_dev = (z * 4 + qa, core), (z * 4 + qb, core)
    own_order, their_order = (qd, qa, qb, col), (qd, qb, qa, col)
    chunks = list(range(depth - 1, 0, -1)) + [0]
    pieces = [(section, dz) for section in (1, 0) for dz in chunks]
    swaps, first, final, last = {}, {}, {}, {}

    def mine(section, q, dz):
        return grads.at[section, core, q, z_at[dz]]

    def add(target, source):
        target[...] = target[...] + source[...]

    def swap(section):
        for dz in chunks:
            for step in range(4):
                q = their_order[step]
                swaps[section, dz, step] = remote(
                    grads.at[section, other, q, z_at[dz]],
                    inbox0.at[section, q, z_at[dz]],
                    partner,
                )

    def summed(section, dz, step):
        q = own_order[step]
        swaps[section, dz, step].wait_recv()
        target = mine(section, q, dz)
        add(target, inbox0.at[section, q, z_at[dz]])
        return target

    def stage_one(section, dz):
        for step in range(2):
            first[section, dz, step] = remote(
                summed(section, dz, step), inbox1.at[section, step, z_at[dz]], a_dev
            )

    def stage_two(section, dz):
        total = summed(section, dz, 2)
        first[section, dz, 0].wait_recv()
        add(total, inbox1.at[section, 0, z_at[dz]])
        final[section, dz] = remote(total, inbox2.at[section, z_at[dz]], b_dev)

    def stage_three(section, dz):
        total = summed(section, dz, 3)
        first[section, dz, 1].wait_recv()
        add(total, inbox1.at[section, 1, z_at[dz]])
        final[section, dz].wait_recv()
        add(total, inbox2.at[section, z_at[dz]])
        if dz > 0:
            last[section, dz] = remote(total, inbox3.at[section, dz], z_dev[dz])

    def turn_of(turn):
        for lag, stage in ((0, stage_one), (LEAD, stage_two), (LEAD + 1, stage_three)):
            if 0 <= turn - lag < len(pieces):
                stage(*pieces[turn - lag])

    def weight_grad(section, kind):
        if kind == 0:
            term = contract_rows(normed[section], gradpre[section])
        else:
            term = contract_rows(acts[section], cots[section])
        for owner in range(dp):
            grads[section, kind, owner % 4, owner // 4] = term[
                owner * shard : (owner + 1) * shard
            ]

    def grad_preact(section):
        def body(g, carry):
            span = pl.ds(pl.multiple_of(g * joint * rows, rows), joint * rows)
            product = contract_cols(cots[section, span, :], weights[section, 1])
            gradpre[section, span, :] = (product * slopes[section, span, :]).astype(jnp.bfloat16)
            return carry

        lax.fori_loop(0, images // joint, body, 0)

    def grad_normed(section):
        gain_row = pbuf[section, 0]

        def body(g, carry):
            span = pl.ds(pl.multiple_of(g * joint * rows, rows), joint * rows)
            product = contract_cols(gradpre[section, span, :], weights[section, 0])
            for j in range(joint):
                i = g * joint + j
                where = pl.ds(pl.multiple_of(i * rows, rows), rows)
                grad = product[j * rows : (j + 1) * rows] * gain_row
                spread[where, :] = grad
                sums[pl.ds(i, 1), :] = jnp.sum(grad, axis=0, keepdims=True)
                sums[pl.ds(images + i, 1), :] = jnp.sum(
                    grad * unit(section, i), axis=0, keepdims=True
                )
            return carry

        lax.fori_loop(0, images // joint, body, 0)

    grad_preact(1)
    weight_grad(1, 1)
    weight_grad(1, 0)
    swap(1)
    grad_normed(1)
    turn_of(0)
    pull_back(1, 1)
    turn_of(1)
    grad_preact(0)
    turn_of(2)
    weight_grad(0, 1)
    turn_of(3)
    weight_grad(0, 0)
    swap(0)
    for turn in range(4, len(pieces) + LEAD + 1):
        turn_of(turn)
    for section in (1, 0):
        total = mine(section, col, 0)[...]
        for dz in chunks[:-1]:
            last[section, dz].wait_recv()
            total = total + inbox3[section, dz]
        result[section] = total
    closing = remote(result.at[other], closed, partner)
    closing.wait_recv()
    ours, theirs = result[core], closed[...]
    out_ref[0, :, :channels] = jnp.where(core == 0, ours, theirs)
    out_ref[0, :, channels:] = jnp.where(core == 0, theirs, ours)
    for copy in pending:
        copy.wait_send()


def fused_body(latents, noise, timesteps, reward_dir, gain, time_scale, w_in, w_out):
    dp = lax.axis_size("dp")
    depth = dp // 4
    micro_count = timesteps.shape[0]
    images = micro_count // 2
    rows = latents.shape[0] // micro_count
    channels = latents.shape[1]
    shard = w_in.shape[1]
    loss_scale = 1.0 / math.sqrt(dp * latents.shape[0])
    shape = (dp, depth, shard, channels, images, rows, loss_scale)
    total_rows = images * rows
    bf16, f32 = jnp.bfloat16, jnp.float32
    lines = -(-2 * images // 8) * 8
    square = (shard, channels)
    copies = 64 * depth
    vmem = pl.BlockSpec(memory_space=pltpu.VMEM)
    grad_rows = pl.pallas_call(
        functools.partial(step_kernel, shape),
        out_shape=jax.ShapeDtypeStruct((1, shard, 2 * channels), f32),
        in_specs=[vmem] * 4 + [pl.BlockSpec(memory_space=pl.ANY)] * 2
        + [pl.BlockSpec(memory_space=pltpu.SMEM), vmem],
        out_specs=vmem,
        scratch_shapes=[
            pltpu.VMEM((-(-images // 8) * 8, channels), f32),
            pltpu.VMEM((3, -(-images // 8) * 8, 128), f32),
            pltpu.VMEM((2, 4, depth, 2) + square, bf16),
            pltpu.VMEM((2, 2, 1, channels), f32),
            pltpu.VMEM((2, 2, channels, channels), bf16),
            pltpu.VMEM((3, total_rows, channels), bf16),
            pltpu.VMEM((total_rows, channels), bf16),
            pltpu.VMEM((2, total_rows, channels), bf16),
            pltpu.VMEM((2, total_rows, channels), f32),
            pltpu.VMEM((2, total_rows, channels), bf16),
            pltpu.VMEM((2, total_rows, channels), bf16),
            pltpu.VMEM((2, total_rows, channels), bf16),
            pltpu.VMEM((3, lines, channels), f32),
            pltpu.VMEM((3, lines, channels), f32),
            pltpu.VMEM((lines, channels), f32),
            pltpu.VMEM((total_rows, channels), f32),
            pltpu.VMEM((channels, 128), bf16),
            pltpu.VMEM((128, channels), bf16),
            pltpu.VMEM((2, 2, 4, depth) + square, f32),
            pltpu.VMEM((2, 4, depth) + square, f32),
            pltpu.VMEM((2, 2, depth) + square, f32),
            pltpu.VMEM((2, depth) + square, f32),
            pltpu.VMEM((2, depth) + square, f32),
            pltpu.VMEM((2,) + square, f32),
            pltpu.VMEM(square, f32),
            pltpu.SemaphoreType.DMA((copies,)),
            pltpu.SemaphoreType.DMA((copies,)),
            pltpu.SemaphoreType.DMA((6,)),
        ],
        compiler_params=pltpu.CompilerParams(
            collective_id=0, has_side_effects=True, vmem_limit_bytes=60 * 1024 * 1024
        ),
    )(w_in, w_out, gain, time_scale, latents, noise, timesteps, reward_dir)
    return grad_rows


def fits(mesh):
    return mesh.shape["segment"] == 2 and mesh.shape["dp"] % 4 == 0 and mesh.shape["dp"] >= 16


def solution(mesh):
    placed = (
        P("dp", None),
        P("dp", None),
        P("dp"),
        P(),
        P("segment", None),
        P("segment", None),
        P("segment", "dp", None),
        P("segment", "dp", None),
    )
    return jax.shard_map(
        fused_body if fits(mesh) else body, mesh=mesh, in_specs=placed, out_specs=P("segment", "dp", None), check_vma=False
    )
```

```python
import functools
import math

import jax
import jax.numpy as jnp
from jax import lax
from jax.experimental import pallas as pl
from jax.experimental.pallas import tpu as pltpu
from jax.sharding import PartitionSpec as P

GROUPS = 32
NSTEPS = 1000
STRIDE = 20
LEAD = 2


EPS = 1e-05


def passed_along(shard, axis, by):
    length = lax.axis_size(axis)
    pairs = [(i, i + by) for i in range(length) if 0 <= i + by < length]
    return lax.ppermute(shard, axis, pairs)


def group_norm(state_f32, group_count):
    channels = state_f32.shape[1]
    per_group = channels // group_count
    col_mean = jnp.mean(state_f32, axis=0)
    group_mean = jnp.repeat(jnp.mean(col_mean.reshape(group_count, per_group), axis=1), per_group)
    centered = state_f32 - group_mean
    sq_mean = jnp.mean(centered * centered, axis=0)
    variance = jnp.repeat(jnp.mean(sq_mean.reshape(group_count, per_group), axis=1), per_group)
    return centered * lax.rsqrt(variance + EPS)


def time_embed(timestep, channels):
    half_width = channels // 2
    frequencies = jnp.exp(
        -math.log(10000.0) * jnp.arange(half_width).astype(jnp.float32) / half_width
    )
    phases = timestep.astype(jnp.float32) * frequencies
    return jnp.concatenate([jnp.sin(phases), jnp.cos(phases)])


def alpha_bar(timestep):
    value = ((timestep.astype(jnp.float32) + 1.0) / NSTEPS + 0.008) / 1.008 * (math.pi / 2.0)
    return jnp.cos(value) ** 2


def contract_rows(left, right):
    return lax.dot_general(
        left, right, (((0,), (0,)), ((), ())), preferred_element_type=jnp.float32
    )


def contract_cols(left, right):
    return lax.dot_general(
        left, right, (((1,), (1,)), ((), ())), preferred_element_type=jnp.float32
    )


def block_forward(hidden, gain_row, temb, first, second):
    state_f32 = hidden.astype(jnp.float32)
    normed = (group_norm(state_f32, GROUPS) * gain_row).astype(jnp.bfloat16)
    preact = jnp.dot(normed, first, preferred_element_type=jnp.float32) + temb
    activation = jax.nn.silu(preact).astype(jnp.bfloat16)
    result = (state_f32 + jnp.dot(activation, second, preferred_element_type=jnp.float32)).astype(
        jnp.bfloat16
    )
    return (result, normed, preact, activation)


def block_backward(hidden, gain_row, preact, cotangent, first, second):
    grad_act = contract_cols(cotangent, second)
    gate_value = jax.nn.sigmoid(preact)
    grad_pre = (grad_act * gate_value * (1.0 + preact * (1.0 - gate_value))).astype(jnp.bfloat16)
    grad_norm = contract_cols(grad_pre, first)
    _, pullback = jax.vjp(lambda values: group_norm(values, GROUPS), hidden.astype(jnp.float32))
    new_cot = (cotangent.astype(jnp.float32) + pullback(grad_norm * gain_row)[0]).astype(
        jnp.bfloat16
    )
    return (new_cot, grad_pre)


def weight_term(normed, grad_pre, activation, cotangent):
    return jnp.concatenate(
        [contract_rows(normed, grad_pre), contract_rows(activation, cotangent)], axis=1
    )


def sample_head(hidden, latent, noise_block, timestep, reward_dir, loss_scale):
    ab_now = alpha_bar(timestep)
    ab_prev = alpha_bar(timestep - STRIDE)
    coef_a = jnp.sqrt(ab_now)
    coef_b = jnp.sqrt(1.0 - ab_now)
    coef_p = jnp.sqrt(ab_prev)
    coef_q = jnp.sqrt(0.75 * (1.0 - ab_prev))
    coef_r = 0.5 * jnp.sqrt(1.0 - ab_prev)
    noise_pred, pullback = jax.vjp(
        lambda values: group_norm(values, GROUPS), hidden.astype(jnp.float32)
    )
    current = latent.astype(jnp.float32)
    previous = (
        coef_p * (current - coef_b * noise_pred) / coef_a
        + coef_q * noise_pred
        + coef_r * noise_block.astype(jnp.float32)
    )
    squashed = jnp.tanh(previous)
    grad_pred = (
        (coef_q - coef_p * coef_b / coef_a) * reward_dir * (1.0 - squashed * squashed) * loss_scale
    )
    return pullback(grad_pred)[0].astype(jnp.bfloat16)


def put_slot(buffer, value, slot_index):
    return lax.dynamic_update_index_in_dim(buffer, value, slot_index, 0)


def body(latents, noise, timesteps, reward_dir, gain, time_scale, w_in, w_out):
    segments = lax.axis_size("segment")
    segment_index = lax.axis_index("segment")
    last_segment = segments - 1
    micro_count = timesteps.shape[0]
    crop_rows = latents.shape[0] // micro_count
    channels = latents.shape[1]
    loss_scale = 1.0 / math.sqrt(lax.axis_size("dp") * latents.shape[0])
    tick_count = micro_count + segments - 1
    whole_in, whole_out = (
        lax.all_gather(w_in, "dp", axis=1, tiled=True),
        lax.all_gather(w_out, "dp", axis=1, tiled=True),
    )
    first = whole_in[0]
    second = whole_out[0]
    gain_row = gain[0]
    latent_blocks = latents.reshape(micro_count, crop_rows, channels)
    noise_blocks = noise.reshape(micro_count, crop_rows, channels)
    embeds = jax.vmap(lambda values: time_embed(values, channels))(timesteps) * time_scale[0]
    blank = jnp.zeros((crop_rows, channels), jnp.bfloat16)
    blank_stack = jnp.zeros((micro_count, crop_rows, channels), jnp.bfloat16)
    stored = ()

    def forward_tick(tick_index, state_carry):
        incoming, inputs, head_cots, kept = state_carry
        micro_index = tick_index - segment_index
        active = (micro_index >= 0) & (micro_index < micro_count)
        slot_index = jnp.clip(micro_index, 0, micro_count - 1)
        fresh_input = latent_blocks[slot_index]
        hidden = jnp.where(segment_index == 0, fresh_input, incoming)

        def forward_compute(buffers):
            inputs, head_cots, kept = buffers
            result, normed, preact, activation = block_forward(
                hidden, gain_row, embeds[slot_index], first, second
            )
            inputs = put_slot(inputs, hidden, slot_index)
            head_cot = lax.cond(
                segment_index == last_segment,
                lambda: sample_head(
                    result,
                    fresh_input,
                    noise_blocks[slot_index],
                    timesteps[slot_index],
                    reward_dir,
                    loss_scale,
                ),
                lambda: blank,
            )
            head_cots = put_slot(head_cots, head_cot, slot_index)
            return (result, inputs, head_cots, kept)

        def forward_skipped(buffers):
            return (blank, buffers[0], buffers[1], buffers[2])

        result, inputs, head_cots, kept = lax.cond(
            active, forward_compute, forward_skipped, (inputs, head_cots, kept)
        )
        incoming = passed_along(result, "segment", 1)
        return (incoming, inputs, head_cots, kept)

    _, inputs, head_cots, kept = lax.fori_loop(
        0, tick_count, forward_tick, (blank, blank_stack, blank_stack, stored)
    )
    grad_start = ()
    records = (blank_stack, blank_stack, blank_stack, blank_stack)

    def backward_tick(tick_index, state_carry):
        incoming, grad_sum, records = state_carry
        micro_index = tick_index - (last_segment - segment_index)
        active = (micro_index >= 0) & (micro_index < micro_count)
        slot_index = jnp.clip(micro_index, 0, micro_count - 1)
        cotangent = jnp.where(segment_index == last_segment, head_cots[slot_index], incoming)

        def backward_compute(buffers):
            grad_sum, records = buffers
            hidden = inputs[slot_index]
            _, normed, preact, activation = block_forward(
                hidden, gain_row, embeds[slot_index], first, second
            )
            new_cot, grad_pre = block_backward(hidden, gain_row, preact, cotangent, first, second)
            records = (
                put_slot(records[0], normed, slot_index),
                put_slot(records[1], grad_pre, slot_index),
                put_slot(records[2], activation, slot_index),
                put_slot(records[3], cotangent, slot_index),
            )
            return (new_cot, grad_sum, records)

        def backward_skipped(buffers):
            return (blank, buffers[0], buffers[1])

        result, grad_sum, records = lax.cond(
            active, backward_compute, backward_skipped, (grad_sum, records)
        )
        incoming = passed_along(result, "segment", -1)
        return (incoming, grad_sum, records)

    _, grad_sum, records = lax.fori_loop(0, tick_count, backward_tick, (blank, grad_start, records))
    flat = [buffer.reshape(micro_count * crop_rows, channels) for buffer in records]
    full_terms = weight_term(flat[0], flat[1], flat[2], flat[3])
    grad_rows = lax.psum_scatter(full_terms, "dp", scatter_dimension=0, tiled=True)
    return grad_rows[None]


def split_rows(values):
    high = values.astype(jnp.bfloat16).astype(jnp.float32)
    rest = values - high
    middle = rest.astype(jnp.bfloat16).astype(jnp.float32)
    low = rest - middle
    return jnp.concatenate([high, middle, low], axis=0).astype(jnp.bfloat16)


class Pair:
    def __init__(self, copies):
        self.copies = copies

    def start(self):
        for copy in self.copies:
            copy.start()

    def wait_recv(self):
        for copy in self.copies:
            copy.wait_recv()

    def wait_send(self):
        for copy in self.copies:
            copy.wait_send()


def step_kernel(
    shape,
    win_ref,
    wout_ref,
    gain_ref,
    time_ref,
    latent_ref,
    noise_ref,
    times_ref,
    reward_ref,
    out_ref,
    embed_ref,
    coef_ref,
    wbuf,
    pbuf,
    weights,
    states,
    noises,
    normed,
    slopes,
    acts,
    cots,
    gradpre,
    means,
    scales,
    sums,
    spread,
    gather_mat,
    scatter_mat,
    grads,
    inbox0,
    inbox1,
    inbox2,
    inbox3,
    result,
    closed,
    send_sem,
    recv_sem,
    local_sem,
):
    dp, depth, shard, channels, images, rows, loss_scale = shape
    me = lax.axis_index("dp")
    core = lax.axis_index("segment")
    other = 1 - core
    col = lax.rem(me, 4)
    z = me // 4
    qx = col + 1 - 2 * lax.rem(col, 2)
    qy = lax.rem(col + 2, 4)
    qd = 3 - col
    x_dev = (z * 4 + qx, core)
    y_dev = (z * 4 + qy, core)
    partner = (me, other)
    z_at = [lax.rem(z + dz, depth) for dz in range(depth)]
    z_from = [lax.rem(z + depth - dz, depth) for dz in range(depth)]
    z_dev = [(z_at[dz] * 4 + col, core) for dz in range(depth)]
    count = [0]
    pending = []

    def reserve(src, dst, device):
        k = count[0]
        count[0] += 1
        copy = pltpu.make_async_remote_copy(
            src_ref=src,
            dst_ref=dst,
            send_sem=send_sem.at[k],
            recv_sem=recv_sem.at[k],
            device_id=device,
            device_id_type=pl.DeviceIdType.MESH,
        )
        return copy

    def remote(src, dst, device):
        copy = reserve(src, dst, device)
        copy.start()
        pending.append(copy)
        return copy

    base = pl.multiple_of(core * (images * rows), images * rows)
    locals_ = [
        pltpu.make_async_copy(source, target, local_sem.at[k])
        for k, (source, target) in enumerate(
            (
                (win_ref.at[0], wbuf.at[core, col, z, 0]),
                (wout_ref.at[0], wbuf.at[core, col, z, 1]),
                (gain_ref, pbuf.at[core, 0]),
                (time_ref, pbuf.at[core, 1]),
                (latent_ref.at[pl.ds(base, images * rows)], states.at[0]),
                (noise_ref.at[pl.ds(base, images * rows)], noises),
            )
        )
    ]
    for copy in locals_:
        copy.start()

    barrier = pltpu.get_barrier_semaphore()
    friends = [x_dev, y_dev, partner] + z_dev[1:]
    for device in friends:
        pl.semaphore_signal(
            barrier, inc=1, device_id=device, device_id_type=pl.DeviceIdType.MESH
        )
    pl.semaphore_wait(barrier, len(friends))

    def own_shard(device):
        return Pair(
            [
                remote(source.at[0], wbuf.at[core, col, z, kind], device)
                for kind, source in enumerate((win_ref, wout_ref))
            ]
        )

    slots = [(way, hop) for hop in range(depth - 1) for way in (1, -1)]

    def holds(way, hop):
        return z >= hop + 1 if way > 0 else z <= depth - 2 - hop

    def goes_on(way):
        return z <= depth - 2 if way > 0 else z >= 1

    def along(way):
        return (lax.rem(z + depth + way, depth) * 4 + col, core)

    own_x, own_y = own_shard(x_dev), own_shard(y_dev)
    line = {}
    for way in (1, -1):
        line[way, 0] = Pair(
            [
                reserve(source.at[0], wbuf.at[core, col, z, kind], along(way))
                for kind, source in enumerate((win_ref, wout_ref))
            ]
        )

        @pl.when(goes_on(way))
        def _(way=way):
            line[way, 0].start()

    to_core = [
        own_shard(partner),
        remote(gain_ref, pbuf.at[core, 0], partner),
        remote(time_ref, pbuf.at[core, 1], partner),
    ]
    ch = lax.broadcasted_iota(jnp.int32, gather_mat.shape, 0)
    gr = lax.broadcasted_iota(jnp.int32, gather_mat.shape, 1) * (channels // GROUPS)
    inside = (ch >= gr) & (ch < gr + channels // GROUPS)
    gather_mat[...] = jnp.where(inside, 1.0, 0.0).astype(jnp.bfloat16)
    ch = lax.broadcasted_iota(jnp.int32, scatter_mat.shape, 1)
    gr = lax.broadcasted_iota(jnp.int32, scatter_mat.shape, 0) * (channels // GROUPS)
    inside = (ch >= gr) & (ch < gr + channels // GROUPS)
    scatter_mat[...] = jnp.where(inside, 1.0, 0.0).astype(jnp.bfloat16)
    sums[...] = jnp.zeros_like(sums)

    def column(stacked):
        line = lax.broadcasted_iota(jnp.int32, stacked.shape, 0)
        values = jnp.zeros(stacked.shape, jnp.float32)
        for i in range(images):
            values = jnp.where(
                line == i, times_ref[core * images + i].astype(jnp.float32), values
            )
        return values

    half_width = channels // 2
    lane = lax.broadcasted_iota(jnp.int32, embed_ref.shape, 1)
    k_index = jnp.where(lane < half_width, lane, lane - half_width).astype(jnp.float32)
    phases = column(embed_ref) * jnp.exp(-math.log(10000.0) * k_index / half_width)
    embed_ref[...] = jnp.where(lane < half_width, jnp.sin(phases), jnp.cos(phases))
    now = column(coef_ref.at[0])
    ab_now, ab_prev = alpha_bar(now), alpha_bar(now - STRIDE)
    coef_a, coef_b = jnp.sqrt(ab_now), jnp.sqrt(1.0 - ab_now)
    coef_p, coef_q = jnp.sqrt(ab_prev), jnp.sqrt(0.75 * (1.0 - ab_prev))
    coef_ref[0] = coef_p / coef_a
    coef_ref[1] = coef_q - coef_p * coef_b / coef_a
    coef_ref[2] = 0.5 * jnp.sqrt(1.0 - ab_prev)

    spread_x, spread_y, diag, core_sends = {}, {}, {}, {}

    def slot_piece(way, hop, q):
        return wbuf.at[core, q, lax.rem(z + depth - way * (hop + 1), depth)]

    for way, hop in slots:
        piece = slot_piece(way, hop, col)
        spread_x[way, hop] = reserve(piece, piece, x_dev)
        spread_y[way, hop] = reserve(piece, piece, y_dev)
        more = [reserve(piece, piece, partner)]
        if hop + 1 < depth - 1:
            line[way, hop + 1] = reserve(piece, piece, along(way))
        core_sends[way, hop] = more

        @pl.when(holds(way, hop))
        def _(way=way, hop=hop, more=more):
            line[way, hop].wait_recv()
            if hop + 1 < depth - 1:

                @pl.when(goes_on(way))
                def _():
                    line[way, hop + 1].start()

            spread_x[way, hop].start()
            spread_y[way, hop].start()
            more[0].start()

    def forward(from_x, from_y, maker):
        return [
            maker(from_x.at[0], from_x.at[0], y_dev),
            maker(from_y.at[1], from_y.at[1], x_dev),
            maker(from_x, from_x, partner),
            maker(from_y, from_y, partner),
        ]

    own_x.wait_recv()
    own_y.wait_recv()
    own_diag = forward(wbuf.at[core, qx, z], wbuf.at[core, qy, z], remote)
    to_core += own_diag[2:]
    for way, hop in slots:
        batch = forward(slot_piece(way, hop, qx), slot_piece(way, hop, qy), reserve)
        diag[way, hop] = batch[:2]
        core_sends[way, hop] += batch[2:]

        @pl.when(holds(way, hop))
        def _(way=way, hop=hop, batch=batch):
            spread_x[way, hop].wait_recv()
            spread_y[way, hop].wait_recv()
            for copy in batch:
                copy.start()

    for copy in own_diag[:2]:
        copy.wait_recv()
    to_core.append(remote(wbuf.at[core, qd, z], wbuf.at[core, qd, z], partner))
    for way, hop in slots:
        piece = slot_piece(way, hop, qd)
        closing_copy = reserve(piece, piece, partner)
        core_sends[way, hop].append(closing_copy)

        @pl.when(holds(way, hop))
        def _(way=way, hop=hop, closing_copy=closing_copy):
            for copy in diag[way, hop]:
                copy.wait_recv()
            closing_copy.start()

    for way, hop in slots:

        @pl.when(holds(way, hop))
        def _(way=way, hop=hop):
            for copy in core_sends[way, hop]:
                copy.wait_recv()

    for copy in locals_:
        copy.wait()
    for copy in to_core:
        copy.wait_recv()

    for section in range(2):
        for kind in range(2):
            for pair in range(dp // 2):
                q, zz = (2 * pair) % 4, pair // 2
                both = jnp.concatenate(
                    [
                        wbuf[section, q, zz, kind].astype(jnp.float32),
                        wbuf[section, q + 1, zz, kind].astype(jnp.float32),
                    ],
                    axis=0,
                )
                weights[section, kind, 2 * pair * shard : 2 * (pair + 1) * shard, :] = (
                    both.astype(jnp.bfloat16)
                )

    def group_means(values):
        parts = jnp.dot(
            split_rows(values), gather_mat[...], preferred_element_type=jnp.float32
        )
        lines = values.shape[0]
        total = parts[:lines] + parts[lines : 2 * lines] + parts[2 * lines :]
        total = total * (1.0 / (rows * (channels // GROUPS)))
        parts = jnp.dot(
            split_rows(total), scatter_mat[...], preferred_element_type=jnp.float32
        )
        return parts[:lines] + parts[lines : 2 * lines] + parts[2 * lines :]

    def statistics(stage):
        def mean_body(i, carry):
            block = states[stage, pl.ds(i * rows, rows), :].astype(jnp.float32)
            sums[pl.ds(i, 1), :] = jnp.sum(block, axis=0, keepdims=True)
            return carry

        lax.fori_loop(0, images, mean_body, 0)
        means[stage] = group_means(sums[...])

        def square_body(i, carry):
            block = states[stage, pl.ds(i * rows, rows), :].astype(jnp.float32)
            centered = block - means[stage, pl.ds(i, 1), :]
            sums[pl.ds(i, 1), :] = jnp.sum(centered * centered, axis=0, keepdims=True)
            return carry

        lax.fori_loop(0, images, square_body, 0)
        scales[stage] = lax.rsqrt(group_means(sums[...]) + EPS)

    def unit(stage, i):
        block = states[stage, pl.ds(i * rows, rows), :].astype(jnp.float32)
        return (block - means[stage, pl.ds(i, 1), :]) * scales[stage, pl.ds(i, 1), :]

    joint = 2 if images % 2 == 0 else 1
    for section in range(2):
        statistics(section)
        gain_row = pbuf[section, 0]
        time_row = pbuf[section, 1]

        def forward_body(g, carry):
            for j in range(joint):
                i = g * joint + j
                where = pl.ds(pl.multiple_of(i * rows, rows), rows)
                normed[section, where, :] = (unit(section, i) * gain_row).astype(jnp.bfloat16)
            span = pl.ds(pl.multiple_of(g * joint * rows, rows), joint * rows)
            product = jnp.dot(
                normed[section, span, :],
                weights[section, 0],
                preferred_element_type=jnp.float32,
            )
            for j in range(joint):
                i = g * joint + j
                where = pl.ds(pl.multiple_of(i * rows, rows), rows)
                preact = product[j * rows : (j + 1) * rows] + time_row * embed_ref[pl.ds(i, 1), :]
                gate = jax.nn.sigmoid(preact)
                acts[section, where, :] = (preact * gate).astype(jnp.bfloat16)
                slopes[section, where, :] = gate * (1.0 + preact * (1.0 - gate))
            product = jnp.dot(
                acts[section, span, :],
                weights[section, 1],
                preferred_element_type=jnp.float32,
            )
            states[section + 1, span, :] = (
                states[section, span, :].astype(jnp.float32) + product
            ).astype(jnp.bfloat16)
            return carry

        lax.fori_loop(0, images // joint, forward_body, 0)

    statistics(2)

    def head_body(i, carry):
        where = pl.ds(pl.multiple_of(i * rows, rows), rows)
        pred = unit(2, i)
        current = states[0, where, :].astype(jnp.float32)
        fresh = noises[where, :].astype(jnp.float32)
        keep, pull, stir = (coef_ref[j, pl.ds(i, 1), 0:1] for j in range(3))
        squashed = jnp.tanh(keep * current + pull * pred + stir * fresh)
        grad = (1.0 - squashed * squashed) * (reward_ref[...][None] * (pull * loss_scale))
        spread[where, :] = grad
        sums[pl.ds(i, 1), :] = jnp.sum(grad, axis=0, keepdims=True)
        sums[pl.ds(images + i, 1), :] = jnp.sum(grad * pred, axis=0, keepdims=True)
        return carry

    lax.fori_loop(0, images, head_body, 0)

    def pull_back(stage, incoming):
        means_two = group_means(sums[...])
        sums[...] = means_two

        def body(i, carry):
            where = pl.ds(pl.multiple_of(i * rows, rows), rows)
            pulled = scales[stage, pl.ds(i, 1), :] * (
                spread[where, :]
                - sums[pl.ds(i, 1), :]
                - unit(stage, i) * sums[pl.ds(images + i, 1), :]
            )
            if incoming is not None:
                pulled = cots[incoming, where, :].astype(jnp.float32) + pulled
            cots[stage - 1, where, :] = pulled.astype(jnp.bfloat16)
            return carry

        lax.fori_loop(0, images, body, 0)

    pull_back(2, None)

    qa = qx + core * (qy - qx)
    qb = qy + core * (qx - qy)
    a_dev, b_dev = (z * 4 + qa, core), (z * 4 + qb, core)
    own_order, their_order = (qd, qa, qb, col), (qd, qb, qa, col)
    chunks = list(range(depth - 1, 0, -1)) + [0]
    pieces = [(section, dz) for section in (1, 0) for dz in chunks]
    swaps, first, final, last = {}, {}, {}, {}

    def mine(section, q, dz):
        return grads.at[section, core, q, z_at[dz]]

    def add(target, source):
        target[...] = target[...] + source[...]

    def swap(section):
        for dz in chunks:
            for step in range(4):
                q = their_order[step]
                swaps[section, dz, step] = remote(
                    grads.at[section, other, q, z_at[dz]],
                    inbox0.at[section, q, z_at[dz]],
                    partner,
                )

    def summed(section, dz, step):
        q = own_order[step]
        swaps[section, dz, step].wait_recv()
        target = mine(section, q, dz)
        add(target, inbox0.at[section, q, z_at[dz]])
        return target

    def stage_one(section, dz):
        for step in range(2):
            first[section, dz, step] = remote(
                summed(section, dz, step), inbox1.at[section, step, z_at[dz]], a_dev
            )

    def stage_two(section, dz):
        total = summed(section, dz, 2)
        first[section, dz, 0].wait_recv()
        add(total, inbox1.at[section, 0, z_at[dz]])
        final[section, dz] = remote(total, inbox2.at[section, z_at[dz]], b_dev)

    def stage_three(section, dz):
        total = summed(section, dz, 3)
        first[section, dz, 1].wait_recv()
        add(total, inbox1.at[section, 1, z_at[dz]])
        final[section, dz].wait_recv()
        add(total, inbox2.at[section, z_at[dz]])
        if dz > 0:
            last[section, dz] = remote(total, inbox3.at[section, dz], z_dev[dz])

    def turn_of(turn):
        for lag, stage in ((0, stage_one), (LEAD, stage_two), (LEAD + 1, stage_three)):
            if 0 <= turn - lag < len(pieces):
                stage(*pieces[turn - lag])

    def weight_grad(section, kind):
        if kind == 0:
            term = contract_rows(normed[section], gradpre[section])
        else:
            term = contract_rows(acts[section], cots[section])
        for owner in range(dp):
            grads[section, kind, owner % 4, owner // 4] = term[
                owner * shard : (owner + 1) * shard
            ]

    def grad_preact(section):
        def body(g, carry):
            span = pl.ds(pl.multiple_of(g * joint * rows, rows), joint * rows)
            product = contract_cols(cots[section, span, :], weights[section, 1])
            gradpre[section, span, :] = (product * slopes[section, span, :]).astype(jnp.bfloat16)
            return carry

        lax.fori_loop(0, images // joint, body, 0)

    def grad_normed(section):
        gain_row = pbuf[section, 0]

        def body(g, carry):
            span = pl.ds(pl.multiple_of(g * joint * rows, rows), joint * rows)
            product = contract_cols(gradpre[section, span, :], weights[section, 0])
            for j in range(joint):
                i = g * joint + j
                where = pl.ds(pl.multiple_of(i * rows, rows), rows)
                grad = product[j * rows : (j + 1) * rows] * gain_row
                spread[where, :] = grad
                sums[pl.ds(i, 1), :] = jnp.sum(grad, axis=0, keepdims=True)
                sums[pl.ds(images + i, 1), :] = jnp.sum(
                    grad * unit(section, i), axis=0, keepdims=True
                )
            return carry

        lax.fori_loop(0, images // joint, body, 0)

    grad_preact(1)
    weight_grad(1, 1)
    weight_grad(1, 0)
    swap(1)
    grad_normed(1)
    turn_of(0)
    pull_back(1, 1)
    turn_of(1)
    grad_preact(0)
    turn_of(2)
    weight_grad(0, 1)
    turn_of(3)
    weight_grad(0, 0)
    swap(0)
    for turn in range(4, len(pieces) + LEAD + 1):
        turn_of(turn)
    for section in (1, 0):
        total = mine(section, col, 0)[...]
        for dz in chunks[:-1]:
            last[section, dz].wait_recv()
            total = total + inbox3[section, dz]
        result[section] = total
    closing = remote(result.at[other], closed, partner)
    closing.wait_recv()
    ours, theirs = result[core], closed[...]
    out_ref[0, :, :channels] = jnp.where(core == 0, ours, theirs)
    out_ref[0, :, channels:] = jnp.where(core == 0, theirs, ours)
    for copy in pending:
        copy.wait_send()
    for way in (1, -1):

        @pl.when(goes_on(way))
        def _(way=way):
            line[way, 0].wait_send()

    for way, hop in slots:

        @pl.when(holds(way, hop))
        def _(way=way, hop=hop):
            sent = [spread_x[way, hop], spread_y[way, hop]] + diag[way, hop]
            for copy in sent + core_sends[way, hop]:
                copy.wait_send()
            if hop + 1 < depth - 1:

                @pl.when(goes_on(way))
                def _():
                    line[way, hop + 1].wait_send()


def fused_body(latents, noise, timesteps, reward_dir, gain, time_scale, w_in, w_out):
    dp = lax.axis_size("dp")
    depth = dp // 4
    micro_count = timesteps.shape[0]
    images = micro_count // 2
    rows = latents.shape[0] // micro_count
    channels = latents.shape[1]
    shard = w_in.shape[1]
    loss_scale = 1.0 / math.sqrt(dp * latents.shape[0])
    shape = (dp, depth, shard, channels, images, rows, loss_scale)
    total_rows = images * rows
    bf16, f32 = jnp.bfloat16, jnp.float32
    lines = -(-2 * images // 8) * 8
    square = (shard, channels)
    copies = 64 * depth
    vmem = pl.BlockSpec(memory_space=pltpu.VMEM)
    grad_rows = pl.pallas_call(
        functools.partial(step_kernel, shape),
        out_shape=jax.ShapeDtypeStruct((1, shard, 2 * channels), f32),
        in_specs=[vmem] * 4 + [pl.BlockSpec(memory_space=pl.ANY)] * 2
        + [pl.BlockSpec(memory_space=pltpu.SMEM), vmem],
        out_specs=vmem,
        scratch_shapes=[
            pltpu.VMEM((-(-images // 8) * 8, channels), f32),
            pltpu.VMEM((3, -(-images // 8) * 8, 128), f32),
            pltpu.VMEM((2, 4, depth, 2) + square, bf16),
            pltpu.VMEM((2, 2, 1, channels), f32),
            pltpu.VMEM((2, 2, channels, channels), bf16),
            pltpu.VMEM((3, total_rows, channels), bf16),
            pltpu.VMEM((total_rows, channels), bf16),
            pltpu.VMEM((2, total_rows, channels), bf16),
            pltpu.VMEM((2, total_rows, channels), f32),
            pltpu.VMEM((2, total_rows, channels), bf16),
            pltpu.VMEM((2, total_rows, channels), bf16),
            pltpu.VMEM((2, total_rows, channels), bf16),
            pltpu.VMEM((3, lines, channels), f32),
            pltpu.VMEM((3, lines, channels), f32),
            pltpu.VMEM((lines, channels), f32),
            pltpu.VMEM((total_rows, channels), f32),
            pltpu.VMEM((channels, 128), bf16),
            pltpu.VMEM((128, channels), bf16),
            pltpu.VMEM((2, 2, 4, depth) + square, f32),
            pltpu.VMEM((2, 4, depth) + square, f32),
            pltpu.VMEM((2, 2, depth) + square, f32),
            pltpu.VMEM((2, depth) + square, f32),
            pltpu.VMEM((2, depth) + square, f32),
            pltpu.VMEM((2,) + square, f32),
            pltpu.VMEM(square, f32),
            pltpu.SemaphoreType.DMA((copies,)),
            pltpu.SemaphoreType.DMA((copies,)),
            pltpu.SemaphoreType.DMA((6,)),
        ],
        compiler_params=pltpu.CompilerParams(
            collective_id=0, has_side_effects=True, vmem_limit_bytes=60 * 1024 * 1024
        ),
    )(w_in, w_out, gain, time_scale, latents, noise, timesteps, reward_dir)
    return grad_rows


def fits(mesh):
    return mesh.shape["segment"] == 2 and mesh.shape["dp"] % 4 == 0 and mesh.shape["dp"] >= 16


def solution(mesh):
    placed = (
        P("dp", None),
        P("dp", None),
        P("dp"),
        P(),
        P("segment", None),
        P("segment", None),
        P("segment", "dp", None),
        P("segment", "dp", None),
    )
    return jax.shard_map(
        fused_body if fits(mesh) else body, mesh=mesh, in_specs=placed, out_specs=P("segment", "dp", None), check_vma=False
    )
```
